1024 devices in a mesh: gx: 16 (over z_hi, x, core), gy: 64 (over y, z_lo).
Axes of the slice: x: 4, y: 4, z: 32 (z_hi: 2, z_lo: 16; z = z_hi * 16 + z_lo), core: 2. Of those that a mesh axis runs over, the one named last changes fastest.
Arguments:
- density: float32 [1024, 256, 128], P('gx', 'gy'), may hold values from 0.8 to 1.2
- velocity: float32 [3, 1024, 256, 128], P(None, 'gx', 'gy'), may hold values from -1 to 1
- pressure: float32 [1024, 256, 128], P('gx', 'gy'), may hold values from 1.5 to 2.5
- disk_cells: int32 [16, 64, 512], P('gx', 'gy'), may hold values from 0 to 32767, as said below
- disk_count: int32 [16, 64], P('gx', 'gy'), may hold values from 0 to 512, as said below
- fringe_level: int32 [64], replicated, may hold values from 0 to 47
Outputs:
- conserved: float32 [5, 1024, 256, 128], P(None, 'gx', 'gy')
The draws below stay inside these ranges and needn't reach their ends.
Inputs may be any that keep to these rules, and one draw needn't show every extreme that they name: `disk_cells`: distinct within each device block; slot k lies in [k * 64 * 4 * 128 // 512, (k + 1) * 64 * 4 * 128 // 512). `disk_count`: zero on the last device column (precursor); exactly 512 on some farm device block.
All inputs are finite; a program needn't handle non-finite values.
Results may differ from the reference program's by a relative error of at most 0.00002.
Values sent between devices are 32-bit elements; how exact they have to be, the bound alone decides.
A program may use at most 32 MiB of HBM per device.

```python
import jax
import jax.numpy as jnp

CX = 64
CY = 4
NZ = 128
FRINGE = 64
SLOTS = 512
STEPS = 1
COLUMNS = 16
SPANS = 64
NX = 1024
NY = 256
N_GX = 16
N_GY = 64


def draw_disk_cells(key, part):
    stride = CX * CY * NZ // SLOTS
    offsets = jax.random.randint(jax.random.fold_in(key, 11), (COLUMNS, SPANS, SLOTS), 0, stride)
    offsets = offsets.at[0, 0, 0].set(0)
    offsets = offsets.at[0, 0, SLOTS - 1].set(stride - 1)
    slot_base = jnp.arange(SLOTS, dtype=jnp.int32)[None, None, :] * stride
    return (slot_base + offsets).astype(jnp.int32)


def draw_disk_count(key, part):
    counts = jax.random.randint(jax.random.fold_in(key, 21), (COLUMNS, SPANS), SLOTS // 4, SLOTS + 1)
    column_ids = jnp.arange(COLUMNS, dtype=jnp.int32)[:, None]
    span_ids = jnp.arange(SPANS, dtype=jnp.int32)[None, :]
    busiest_column = jax.random.randint(jax.random.fold_in(key, 22), (), 0, COLUMNS - 1)
    busiest_span = jax.random.randint(jax.random.fold_in(key, 23), (), 0, SPANS)
    counts = jnp.where((column_ids == busiest_column) & (span_ids == busiest_span), SLOTS, counts)
    counts = jnp.where(column_ids == COLUMNS - 1, 0, counts)
    return counts.astype(jnp.int32)


def set_ends(values, stream_key, least, largest):
    longest = values.shape.index(max(values.shape))
    spots = []
    for shift in (0, 1):
        where = [jax.random.randint(jax.random.fold_in(stream_key, axis), (), 0, length) for axis, length in enumerate(values.shape)]
        where[longest] = (where[longest] + shift) % values.shape[longest]
        spots.append(tuple(where))
    return values.at[spots[0]].set(least).at[spots[1]].set(largest)


def level_of(stream_key, extent, pieces, low, high):
    loudness = 1.0
    for dim, blocks in pieces:
        steps = jax.random.uniform(jax.random.fold_in(jax.random.fold_in(stream_key, 6), dim), (blocks,), jnp.float32, low / len(pieces), high / len(pieces))
        loudness = loudness * jnp.repeat(jnp.exp(steps), extent[dim] // blocks).reshape((-1,) + (1,) * (len(extent) - 1 - dim))
    return loudness


def gaussian(stream_key, dims, deviation, reach, pieces=(), kind=jnp.bfloat16):
    array = jax.random.normal(stream_key, dims, jnp.float32) * deviation
    if len(pieces) > 0:
        array = level_of(stream_key, dims, pieces, -0.22, 0.18) * array
    return jnp.clip(array, min=-reach, max=reach).astype(kind)


def setup_inputs(seed: int = 0) -> dict:
    arg_keys = jax.random.split(jax.random.key(seed), 7)
    density = jnp.clip(0.8 + 0.40000004 * jax.random.uniform(arg_keys[0], (NX, NY, NZ), jnp.float32) ** level_of(arg_keys[0], (NX, NY, NZ), ((0, 16), (1, 64)), -0.2, 0.2), 0.8, 1.2)
    velocity = gaussian(arg_keys[1], (3, NX, NY, NZ), 0.3, 1.0, ((1, 16), (2, 64)), jnp.float32)
    pressure = jnp.clip(1.5 + 1.0 * jax.random.uniform(arg_keys[2], (NX, NY, NZ), jnp.float32) ** level_of(arg_keys[2], (NX, NY, NZ), ((0, 16), (1, 64)), -0.2, 0.2), 1.5, 2.5)
    disk_cells = draw_disk_cells(jax.random.fold_in(arg_keys[6], 71), 0)
    disk_count = draw_disk_count(jax.random.fold_in(arg_keys[6], 71), 0)
    fringe_level = set_ends(jax.random.randint(arg_keys[5], (FRINGE,), 0, 48), jax.random.fold_in(arg_keys[5], 1), 0, 47).astype(jnp.int32)
    return dict(density=density, velocity=velocity, pressure=pressure, disk_cells=disk_cells, disk_count=disk_count, fringe_level=fringe_level)


TIME_STEP = 0.05
VISCOSITY = 0.5
THRUST_COEFF = 0.75
MEAN_WIND = 1.0


def flux_along(fields, direction):
    density = fields[0]
    speeds = fields[1:4] / density
    pressure = 0.4 * (fields[4] - 0.5 * (fields[1] * speeds[0] + fields[2] * speeds[1] + fields[3] * speeds[2]))
    carried = speeds[direction]
    parts = [fields[1 + direction], fields[1] * carried, fields[2] * carried, fields[3] * carried, (fields[4] + pressure) * carried]
    parts[1 + direction] = parts[1 + direction] + pressure
    return jnp.stack(parts)


def vertical_pair(values):
    upper = jnp.concatenate([values[..., 1:], values[..., -1:]], axis=-1)
    lower = jnp.concatenate([values[..., :1], values[..., :-1]], axis=-1)
    return upper, lower


def add_terms(tendency_sum, fields, upper_flux, lower_flux, upper_cells, lower_cells):
    return tendency_sum - 0.5 * (upper_flux - lower_flux) + VISCOSITY * (upper_cells + lower_cells - 2.0 * fields)


def conserved_from(density, velocity, pressure):
    stream = velocity[0] + MEAN_WIND
    energy = pressure / 0.4 + 0.5 * density * (stream * stream + velocity[1] * velocity[1] + velocity[2] * velocity[2])
    return jnp.stack([density, density * stream, density * velocity[1], density * velocity[2], energy])


def stream_pair(values, boundary):
    total = values.shape[1]
    upper = jnp.concatenate([values[:, 1:boundary], values[:, boundary - 1:boundary], values[:, boundary + 1:], values[:, boundary:boundary + 1]], axis=1)
    lower = jnp.concatenate([values[:, total - 1:total], values[:, 0:boundary - 1], values[:, total - 1:total], values[:, boundary:total - 1]], axis=1)
    return upper, lower


def tendency(fields, spot_x, spot_y, spot_z, active, boundary):
    tendency_sum = jnp.zeros_like(fields)
    moved = flux_along(fields, 0)
    upper_flux, lower_flux = stream_pair(moved, boundary)
    upper_cells, lower_cells = stream_pair(fields, boundary)
    tendency_sum = add_terms(tendency_sum, fields, upper_flux, lower_flux, upper_cells, lower_cells)
    moved = flux_along(fields, 1)
    tendency_sum = add_terms(tendency_sum, fields, jnp.roll(moved, -1, axis=2), jnp.roll(moved, 1, axis=2), jnp.roll(fields, -1, axis=2), jnp.roll(fields, 1, axis=2))
    moved = flux_along(fields, 2)
    upper_flux, lower_flux = vertical_pair(moved)
    upper_cells, lower_cells = vertical_pair(fields)
    tendency_sum = add_terms(tendency_sum, fields, upper_flux, lower_flux, upper_cells, lower_cells)
    rho_at = fields[0][spot_x, spot_y, spot_z]
    stream_at = fields[1][spot_x, spot_y, spot_z] / rho_at
    force = -0.5 * THRUST_COEFF * rho_at * stream_at * jnp.abs(stream_at) * active
    tendency_sum = tendency_sum.at[1, spot_x, spot_y, spot_z].add(force)
    tendency_sum = tendency_sum.at[4, spot_x, spot_y, spot_z].add(force * stream_at)
    return tendency_sum


def blend(fields, weights, boundary):
    inlet_cells = fields[:, 0:FRINGE]
    source = fields[:, boundary:boundary + FRINGE]
    blended = inlet_cells + weights[None, :, None, None] * (source - inlet_cells)
    return fields.at[:, 0:FRINGE].set(blended)


def reference(density, velocity, pressure, disk_cells, disk_count, fringe_level):
    boundary = (N_GX - 1) * CX
    fields = conserved_from(density, velocity, pressure)
    column_ids = jnp.arange(N_GX, dtype=jnp.int32)[:, None, None]
    span_ids = jnp.arange(N_GY, dtype=jnp.int32)[None, :, None]
    spot_x = (column_ids * CX + disk_cells // (CY * NZ)).reshape(-1).astype(jnp.int32)
    spot_y = (span_ids * CY + (disk_cells // NZ) % CY).reshape(-1).astype(jnp.int32)
    spot_z = (disk_cells % NZ).reshape(-1).astype(jnp.int32)
    slot_ids = jnp.arange(SLOTS, dtype=jnp.int32)[None, None, :]
    active = (slot_ids < disk_count[:, :, None]).astype(jnp.float32).reshape(-1)
    weights = fringe_level.astype(jnp.float32) / 64.0
    for step_index in range(STEPS):
        first = blend(fields + TIME_STEP * tendency(fields, spot_x, spot_y, spot_z, active, boundary), weights, boundary)
        second = blend(0.75 * fields + 0.25 * (first + TIME_STEP * tendency(first, spot_x, spot_y, spot_z, active, boundary)), weights, boundary)
        fields = blend(fields / 3.0 + (2.0 / 3.0) * (second + TIME_STEP * tendency(second, spot_x, spot_y, spot_z, active, boundary)), weights, boundary)
    return fields
```

```python
import jax
import jax.numpy as jnp
from jax import lax
from jax.experimental import pallas as pl
from jax.experimental.pallas import tpu as pltpu
from jax.sharding import PartitionSpec as P

TIME_STEP = 0.05
THRUST_COEFF = 0.75
MEAN_WIND = 1.0
MESH = pl.DeviceIdType.MESH

CX, CY, NZ, NF = 64, 4, 128, 5
HY = 3
ROWS = CY + 2 * HY
XT = CX // 8 + 2
EX = 8 * XT
LAST = 15
Z_LO = 16


def conserved_from(density, velocity, pressure):
    stream = velocity[0] + MEAN_WIND
    energy = pressure / 0.4 + 0.5 * density * (
        stream * stream + velocity[1] * velocity[1] + velocity[2] * velocity[2]
    )
    return jnp.stack(
        [density, density * stream, density * velocity[1], density * velocity[2], energy]
    )


def body(s_ref, d_ref, w_ref, o_ref, st, ax, bx, ay, by, rr, thrust, dn, ra, rb, rbl, rbr,
         local_sem, send_sem, recv_sem):
    gx, gy = lax.axis_index("gx"), lax.axis_index("gy")
    up, down = lax.rem(gy + 1, 64), lax.rem(gy + 63, 64)
    z_lo = lax.rem(gy, Z_LO)
    first_z, last_z = z_lo == 0, z_lo == Z_LO - 1
    has_right, has_left = gx <= LAST - 2, (gx >= 1) & (gx <= LAST - 1)
    from_left, from_right = (gx >= 1) & (gx <= LAST - 1), gx <= LAST - 2
    u0 = st.at[0, 0]
    p0 = st.at[1, 0]

    sends = []

    def remote(index, recv, src, dst, target):
        return pltpu.make_async_remote_copy(
            src_ref=src, dst_ref=dst, send_sem=send_sem.at[index], recv_sem=recv_sem.at[recv],
            device_id=target, device_id_type=MESH,
        )

    barrier = pltpu.get_barrier_semaphore()

    def tell(condition, device):
        @pl.when(condition)
        def _():
            pl.semaphore_signal(barrier, inc=1, device_id=device, device_id_type=MESH)

    always = gx >= 0
    is_source = gx == LAST
    is_a = (gx == 9) | (gx == 11) | (gx == 13)
    is_b = (gx == 1) | (gx == 3) | (gx == 5) | (gx == 7)
    tell(is_b & (gx == 7), (LAST + 0 * gx, gy))
    tell(is_b & (gx != 7), (gx + 8, gy))
    tell((gx == 7) & first_z, (LAST + 0 * gx, down))
    tell(((gx == 3) | (gx == 5)) & first_z, (gx + 8, down))
    tell(((gx == 1) | (gx == 3) | (gx == 5)) & last_z, (gx + 8, up))
    tell(always, (gx, up))
    tell(always, (gx, down))
    for near in (gy, up, down):
        tell(from_left, (gx - 1, near))
        tell(from_right, (gx + 1, near))
    tell(is_a, (LAST + 0 * gx, gy))
    for c in range(4):
        tell(gx == 0, (1 + 2 * c + 0 * gx, gy))
        if c >= 1:
            tell((gx == 0) & jnp.logical_not(first_z), (1 + 2 * c + 0 * gx, down))
        if c <= 2:
            tell((gx == 0) & jnp.logical_not(last_z), (1 + 2 * c + 0 * gx, up))

    own = pltpu.make_async_copy(s_ref, u0.at[pl.ds(HY, CY), :, pl.ds(8, CX)], local_sem)
    own.start()

    def yes(condition):
        return jnp.where(condition, 1, 0)

    expected = 2 + 3 * yes(has_right) + 3 * yes(has_left)
    expected += yes(is_source) * (4 + yes(last_z))
    expected += yes(is_a) * (1 + yes(first_z)) + yes((gx == 11) | (gx == 13)) * yes(last_z)
    expected += yes(is_b)
    expected += yes((gx >= 3) & is_b) * yes(jnp.logical_not(last_z))
    expected += yes((gx <= 5) & is_b) * yes(jnp.logical_not(first_z))
    pl.semaphore_wait(barrier, expected)

    def send(condition, copy):
        sends.append((condition, copy))

        @pl.when(condition)
        def _():
            copy.start()

    send(is_source, remote(16, 17, s_ref.at[3], rb, (7 + 0 * gx, gy)))
    for c in range(3):
        send(is_source, remote(17 + c, 16, s_ref.at[c], ra, (9 + 2 * c + 0 * gx, gy)))
    send(is_source & last_z, remote(20, 18, s_ref.at[3], rbl, (7 + 0 * gx, up)))

    lo8, hi8 = pl.ds(0, 8), pl.ds(CX - 8, 8)
    left8, right8, mid = pl.ds(0, 8), pl.ds(EX - 8, 8), pl.ds(8, CX)
    halo = [
        (always, s_ref.at[pl.ds(1, 3)], u0.at[pl.ds(0, 3), :, mid], (gx, up), always, (0, 1)),
        (always, s_ref.at[pl.ds(0, 3)], u0.at[pl.ds(7, 3), :, mid], (gx, down), always, (2, 1)),
        (has_right, s_ref.at[:, :, hi8], u0.at[pl.ds(3, 4), :, left8], (gx + 1, gy), from_left, (1, 0)),
        (has_left, s_ref.at[:, :, lo8], u0.at[pl.ds(3, 4), :, right8], (gx - 1, gy), from_right, (1, 2)),
        (has_right, s_ref.at[pl.ds(2, 2), :, hi8], u0.at[pl.ds(1, 2), :, left8], (gx + 1, up), from_left, (0, 0)),
        (has_right, s_ref.at[pl.ds(0, 2), :, hi8], u0.at[pl.ds(7, 2), :, left8], (gx + 1, down), from_left, (2, 0)),
        (has_left, s_ref.at[pl.ds(2, 2), :, lo8], u0.at[pl.ds(1, 2), :, right8], (gx - 1, up), from_right, (0, 2)),
        (has_left, s_ref.at[pl.ds(0, 2), :, lo8], u0.at[pl.ds(7, 2), :, right8], (gx - 1, down), from_right, (2, 2)),
    ]
    receipts = []
    for i, (condition, src, dst, target, arrives, place) in enumerate(halo):
        big = remote(i, i, src, dst, target)
        small = remote(8 + i, 8 + i, d_ref, dn.at[place[0], place[1]], target)
        send(condition, big)
        send(condition, small)
        receipts.append((arrives, big))
        receipts.append((arrives, small))

    @pl.when(is_a)
    def _():
        remote(17, 16, ra, ra, (gx, gy)).wait_recv()

    send(is_a, remote(21, 17, ra, rb, (gx - 8, gy)))
    send(((gx == 11) | (gx == 13)) & last_z, remote(22, 18, ra, rbl, (gx - 8, up)))
    send(is_a & first_z, remote(23, 19, ra, rbr, (gx - 8, down)))

    @pl.when(is_b)
    def _():
        remote(16, 17, rb, rb, (gx, gy)).wait_recv()

    for c in range(4):
        b = gx == 1 + 2 * c
        send(b, remote(24, 20 + HY + c, rb, p0.at[HY + c, :, mid], (0 * gx, gy)))
        if c >= 1:
            send(b & jnp.logical_not(last_z), remote(25, 20 + c - 1, rb, p0.at[c - 1, :, mid], (0 * gx, up)))
        if c <= 2:
            send(b & jnp.logical_not(first_z), remote(26, 20 + 7 + c, rb, p0.at[7 + c, :, mid], (0 * gx, down)))
    for c in range(1, 4):
        b = (gx == 1 + 2 * c) & first_z

        @pl.when(b)
        def _():
            remote(20, 18, rbl, rbl, (gx, gy)).wait_recv()

        send(b, remote(27, 20 + c - 1, rbl, p0.at[c - 1, :, mid], (0 * gx, gy)))
    for c in range(3):
        b = (gx == 1 + 2 * c) & last_z

        @pl.when(b)
        def _():
            remote(23, 19, rbr, rbr, (gx, gy)).wait_recv()

        send(b, remote(28, 20 + 7 + c, rbr, p0.at[7 + c, :, mid], (0 * gx, gy)))

    @pl.when(gx == 0)
    def _():
        for r in range(ROWS):
            remote(24, 20 + r, rb, p0.at[r, :, mid], (gx, gy)).wait_recv()

    strip = pl.ds(1, 8)
    for k, (a, b) in enumerate(((64, 0), (8, 8))):
        copy = remote(29 + k, 30 + k, p0.at[strip, :, pl.ds(a, 8)], p0.at[strip, :, pl.ds(b, 8)], (1 + 0 * gx, gy))
        send(gx == 0, copy)

        @pl.when(gx == 1)
        def _(copy=copy):
            copy.wait_recv()

    own.wait()
    for condition, copy in receipts:
        @pl.when(condition)
        def _(copy=copy):
            copy.wait_recv()
    for condition, copy in sends:
        @pl.when(condition)
        def _(copy=copy):
            copy.wait_send()

    @pl.when(gx == 0)
    def _():
        @pl.loop(0, ROWS)
        def _(r):
            p0[r, :, 0:8] = p0[r, :, 64:72]
            p0[r, :, 72:80] = p0[r, :, 8:16]
            u0[r, :, 0:8] = p0[r, :, 64:72]

    @pl.when(gx == LAST)
    def _():
        @pl.loop(0, ROWS)
        def _(r):
            u0[r, :, 0:8] = u0[r, :, 64:72]
            u0[r, :, 72:80] = u0[r, :, 8:16]

    dn[1, 1] = d_ref[...]
    lane = lax.broadcasted_iota(jnp.int32, (8, NZ), 1)
    lane_f = lane.astype(jnp.float32)
    for ny in range(3):
        rows = {0: (1, 2, 3), 1: (0, 1, 2, 3), 2: (0, 1, 2)}[ny]
        base = {0: -1, 1: 3, 2: 7}[ny]
        for nx in range(3):
            spots = jnp.transpose(dn[ny, nx])
            if nx == 0:
                spots = jnp.where(from_left, spots[CX - 8:CX], -1.0)
            elif nx == 1:
                spots = spots[:CX]
            else:
                spots = jnp.where(from_right, spots[0:8], -1.0)
            start = {0: 0, 1: 8, 2: EX - 8}[nx]
            for y in rows:
                for t in range(spots.shape[0] // 8):
                    one = spots[8 * t:8 * t + 8, 2 * y:2 * y + 1]
                    two = spots[8 * t:8 * t + 8, 2 * y + 1:2 * y + 2]
                    hit = (lane_f == one) | (lane_f == two)
                    thrust[base + y, start + 8 * t:start + 8 * t + 8] = jnp.where(hit, -0.5 * THRUST_COEFF, 0.0)

    low_edge, high_edge = lane == 0, lane == NZ - 1

    def terms(which, slot, row, t):
        cells = pl.ds(pl.multiple_of(8 * t, 8), 8)
        shifted = pl.ds(pl.multiple_of(8 * t + 8, 8), 8)
        u = [st[which, slot, row, f, cells] for f in range(NF)]
        inverse = 1.0 / u[0]
        speed = [u[1] * inverse, u[2] * inverse, u[3] * inverse]
        pressure = 0.4 * (u[4] - 0.5 * (u[1] * speed[0] + u[2] * speed[1] + u[3] * speed[2]))
        total = u[4] + pressure
        flux = []
        for d in range(3):
            part = [u[1 + d], u[1] * speed[d], u[2] * speed[d], u[3] * speed[d], total * speed[d]]
            part[1 + d] = part[1 + d] + pressure
            flux.append(part)
        if which == 0:
            force = thrust[row, cells] * u[1] * jnp.abs(speed[0])
        for f in range(NF):
            ax[row, f, shifted] = u[f] + flux[0][f]
            bx[row, f, shifted] = u[f] - flux[0][f]
            ay[row, f, cells] = u[f] + flux[1][f]
            by[row, f, cells] = u[f] - flux[1][f]
            a, b = u[f] + flux[2][f], u[f] - flux[2][f]
            vertical = jnp.where(low_edge, a, pltpu.roll(a, 1, 1)) + jnp.where(high_edge, b, pltpu.roll(b, NZ - 1, 1))
            rest = 0.5 * vertical - 3.0 * u[f]
            if which == 0 and f == 1:
                rest = rest + force
            if which == 0 and f == 4:
                rest = rest + force * speed[0]
            rr[row, f, cells] = rest

    def update(which, slot, row, t, keep, take):
        cells = pl.ds(pl.multiple_of(8 * t, 8), 8)
        for f in range(NF):
            near = ax[row, f, pl.ds(8 * t + 7, 8)] + bx[row, f, pl.ds(8 * t + 9, 8)]
            near = near + (ay[row - 1, f, cells] + by[row + 1, f, cells])
            slope = 0.5 * near + rr[row, f, cells]
            fresh = st[which, slot, row, f, cells] + TIME_STEP * slope
            st[which, 1, row, f, cells] = keep * st[which, 0, row, f, cells] + take * fresh

    def stage(s, carry):
        slot = jnp.minimum(s, 1)
        keep = jnp.where(s == 0, 0.0, jnp.where(s == 1, 0.75, 1.0 / 3.0))
        take = jnp.where(s == 0, 1.0, jnp.where(s == 1, 0.25, 2.0 / 3.0))

        def advance(which, tiles):
            @pl.loop(s, ROWS - s)
            def _(row):
                @pl.loop(0, tiles)
                def _(t):
                    terms(which, slot, row, t)

            if which == 0:
                @pl.when(gx == LAST - 1)
                def _():
                    @pl.loop(s, ROWS - s)
                    def _(row):
                        bx[row, :, 80:81] = bx[row, :, 79:80]

            @pl.loop(s + 1, ROWS - 1 - s)
            def _(row):
                @pl.loop(0, tiles)
                def _(t):
                    update(which, slot, row, t, keep, take)

        @pl.when(gx <= 1)
        def _():
            advance(1, jnp.where(gx == 0, XT, 2))

        advance(0, XT)

        @pl.when(gx <= 1)
        def _():
            @pl.loop(s + 1, ROWS - 1 - s)
            def _(row):
                @pl.loop(0, jnp.where(gx == 0, XT - 1, 1))
                def _(t):
                    cells = pl.ds(pl.multiple_of(8 * t, 8), 8)
                    weight = w_ref[cells]
                    for f in range(NF):
                        value = st[0, 1, row, f, cells]
                        st[0, 1, row, f, cells] = value + weight * (st[1, 1, row, f, cells] - value)

        return carry

    lax.fori_loop(0, 3, stage, 0)
    for y in range(CY):
        o_ref[y] = st[0, 1, HY + y, :, 8:8 + CX]


def shards(density, velocity, pressure, disk_cells, disk_count, fringe_level):
    column = lax.axis_index("gx")
    with jax.named_scope("state"):
        fields = conserved_from(density, velocity, pressure)
        fields = jnp.transpose(fields, (2, 0, 1, 3))
    with jax.named_scope("disks"):
        cells = disk_cells.reshape(-1)
        slots = jnp.arange(cells.shape[0], dtype=jnp.int32)
        spots = jnp.where(slots < disk_count.reshape(()), cells % NZ, -1).astype(jnp.float32)
        spots = jnp.transpose(spots.reshape(CX, 2 * CY))
        spots = jnp.pad(spots, ((0, 0), (0, NZ - CX)), constant_values=-1.0)
    with jax.named_scope("fringe"):
        weights = fringe_level.astype(jnp.float32) / 64.0
        one, zero = jnp.ones((8,), jnp.float32), jnp.zeros((8,), jnp.float32)
        at_first = jnp.concatenate([one, weights, zero])
        at_second = jnp.concatenate([weights[CX - 8:], jnp.zeros((EX - 8,), jnp.float32)])
        weights = jnp.where(column == 0, at_first, jnp.where(column == 1, at_second, 0.0))
        weights = jnp.broadcast_to(weights[:, None], (EX, NZ))
    vmem = pl.BlockSpec(memory_space=pltpu.VMEM)
    f32 = jnp.float32
    out = pl.pallas_call(
        body,
        out_shape=jax.ShapeDtypeStruct((CY, NF, CX, NZ), f32),
        in_specs=[vmem, vmem, vmem],
        out_specs=vmem,
        scratch_shapes=[
            pltpu.VMEM((2, 2, ROWS, NF, EX, NZ), f32),
            pltpu.VMEM((ROWS, NF, EX + 16, NZ), f32),
            pltpu.VMEM((ROWS, NF, EX + 16, NZ), f32),
            pltpu.VMEM((ROWS, NF, EX, NZ), f32),
            pltpu.VMEM((ROWS, NF, EX, NZ), f32),
            pltpu.VMEM((ROWS, NF, EX, NZ), f32),
            pltpu.VMEM((ROWS, EX, NZ), f32),
            pltpu.VMEM((3, 3, 8, NZ), f32),
            pltpu.VMEM((NF, CX, NZ), f32),
            pltpu.VMEM((NF, CX, NZ), f32),
            pltpu.VMEM((NF, CX, NZ), f32),
            pltpu.VMEM((NF, CX, NZ), f32),
            pltpu.SemaphoreType.DMA,
            pltpu.SemaphoreType.DMA((32,)),
            pltpu.SemaphoreType.DMA((32,)),
        ],
        compiler_params=pltpu.CompilerParams(collective_id=0, has_side_effects=True),
    )(fields, spots, weights)
    return jnp.transpose(out, (1, 2, 0, 3))


def solution(mesh):
    in_specs = (
        P("gx", "gy", None),
        P(None, "gx", "gy", None),
        P("gx", "gy", None),
        P("gx", "gy", None),
        P("gx", "gy"),
        P(),
    )
    out_specs = P(None, "gx", "gy", None)
    return jax.shard_map(shards, mesh=mesh, in_specs=in_specs, out_specs=out_specs, check_vma=False)
```

```python
import jax
import jax.numpy as jnp
from jax import lax
from jax.experimental import pallas as pl
from jax.experimental.pallas import tpu as pltpu
from jax.sharding import PartitionSpec as P

TIME_STEP = 0.05
THRUST_COEFF = 0.75
MEAN_WIND = 1.0
MESH = pl.DeviceIdType.MESH

CX, CY, NZ, NF = 64, 4, 128, 5
HY = 3
ROWS = CY + 2 * HY
XT = CX // 8 + 2
EX = 8 * XT
LAST = 15
Z_LO = 16


def conserved_from(density, velocity, pressure):
    stream = velocity[0] + MEAN_WIND
    energy = pressure / 0.4 + 0.5 * density * (
        stream * stream + velocity[1] * velocity[1] + velocity[2] * velocity[2]
    )
    return jnp.stack(
        [density, density * stream, density * velocity[1], density * velocity[2], energy]
    )


HX = 3
SUB = 4
PIECE = CX // SUB


def body(s_ref, d_ref, count_ref, level_ref, o_ref, st, ax, bx, ay, by, rr, thrust, wt, dd, dn, ra, rb, rbl, rbr,
         go_sem, local_sem, send_sem, recv_sem):
    gx, gy = lax.axis_index("gx"), lax.axis_index("gy")
    up, down = lax.rem(gy + 1, 64), lax.rem(gy + 63, 64)
    z_lo = lax.rem(gy, Z_LO)
    first_z, last_z = z_lo == 0, z_lo == Z_LO - 1
    has_right, has_left = gx <= LAST - 2, (gx >= 1) & (gx <= LAST - 1)
    from_left, from_right = (gx >= 1) & (gx <= LAST - 1), gx <= LAST - 2
    u0 = st.at[0, 0]
    p0 = st.at[1, 0]
    zero = 0 * gx

    sends = []
    numbers = iter(range(1000))

    def remote(send_index, recv, src, dst, target):
        return pltpu.make_async_remote_copy(
            src_ref=src, dst_ref=dst, send_sem=send_sem.at[send_index], recv_sem=recv_sem.at[recv],
            device_id=target, device_id_type=MESH,
        )

    def send(condition, recv, src, dst, target):
        copy = remote(next(numbers), recv, src, dst, target)
        sends.append((condition, copy))

        @pl.when(condition)
        def _():
            copy.start()

        return copy

    def arrived(recv, dst):
        remote(0, recv, dst, dst, (gx, gy)).wait_recv()

    barrier = pltpu.get_barrier_semaphore()

    def tell(condition, device):
        @pl.when(condition)
        def _():
            pl.semaphore_signal(barrier, inc=1, device_id=device, device_id_type=MESH)

    always = gx >= 0
    is_source = gx == LAST
    near_source = (9, 11, 13, 14)
    near_fringe = (1, 3, 5, 7)
    for c in range(4):
        a, b = near_source[c], near_fringe[c]
        tell(gx == b, (a + zero, gy))
        if c >= 1:
            tell((gx == b) & first_z, (a + zero, down))
        if c <= 2:
            tell((gx == b) & last_z, (a + zero, up))
    at_step = first_z | last_z
    not_first, not_last = jnp.logical_not(first_z), jnp.logical_not(last_z)
    tell(not_last, (gx, up))
    tell(not_first, (gx, down))
    for near, close in ((gy, always), (up, not_last), (down, not_first)):
        tell(from_left & (close | (gx == 8)), (gx - 1, near))
        tell(from_right & (close | (gx == 7)), (gx + 1, near))
    half = jnp.where(gx < 8, 0, 8)
    speaker = jnp.where(gx < 8, 7, 8)
    tell(last_z, (speaker, up))
    tell(first_z, (speaker, down))
    tell(at_step & (gx != speaker), (speaker, gy))
    for c in range(4):
        tell(gx == near_source[c], (LAST + zero, gy))
        tell(gx == 0, (near_fringe[c] + zero, gy))

    own = pltpu.make_async_copy(s_ref, u0.at[pl.ds(HY, CY), :, pl.ds(8, CX)], local_sem)
    own.start()

    slot = NZ * lax.broadcasted_iota(jnp.int32, (4, NZ), 0) + lax.broadcasted_iota(jnp.int32, (4, NZ), 1)
    spots = jnp.where(slot < count_ref[0, 0], d_ref[...] & (NZ - 1), -1).astype(jnp.float32)
    dd[0:4] = spots
    dd[4:8] = spots

    def yes(condition):
        return jnp.where(condition, 1, 0)

    is_a = (gx == 9) | (gx == 11) | (gx == 13) | (gx == 14)
    is_b = (gx == 1) | (gx == 3) | (gx == 5) | (gx == 7)
    near_count = 3 - yes(at_step)
    expected = near_count - 1 + 4 * yes(is_source) + yes(is_a) + yes(is_b)
    expected += yes(has_right) * jnp.where(gx == 7, 3, near_count)
    expected += yes(has_left) * jnp.where(gx == 8, 3, near_count)
    expected += 15 * yes(at_step & (gx == speaker))
    expected += yes(is_a & (gx >= 11) & last_z) + yes(is_a & (gx <= 13) & first_z)
    pl.semaphore_wait(barrier, expected)
    for k in range(8):
        @pl.when(at_step & (gx == speaker) & (gx != half + k))
        def _(k=k):
            pl.semaphore_signal(go_sem, inc=1, device_id=(half + k, gy), device_id_type=MESH)

    at_ra, at_rb, at_rbl, at_rbr, at_p = 16, 16 + SUB, 16 + 2 * SUB, 16 + 3 * SUB, 16 + 4 * SUB
    at_strip = at_p + ROWS * SUB
    pieces = [pl.ds(PIECE * j, PIECE) for j in range(SUB)]
    inner = [pl.ds(8 + PIECE * j, PIECE) for j in range(SUB)]

    for j in range(SUB):
        for c in range(4):
            send(is_source, at_ra + j, s_ref.at[c, :, pieces[j]], ra.at[:, pieces[j]], (near_source[c] + zero, gy))

    @pl.when(is_a)
    def _():
        for j in range(SUB):
            arrived(at_ra + j, ra.at[:, pieces[j]])
    target = gx - 8 + yes(gx == 14)
    for j in range(SUB):
        piece = ra.at[:, pieces[j]]
        send(is_a, at_rb + j, piece, rb.at[:, pieces[j]], (target, gy))
        send(is_a & (gx >= 11) & last_z, at_rbl + j, piece, rbl.at[:, pieces[j]], (target, up))
        send(is_a & (gx <= 13) & first_z, at_rbr + j, piece, rbr.at[:, pieces[j]], (target, down))
    rows_out = sends[4 * SUB:]
    del sends[4 * SUB:]
    for condition, copy in rows_out:
        @pl.when(condition)
        def _(copy=copy):
            copy.wait_send()

    mid = pl.ds(8, CX)
    def edge(first, rows, low, cells):
        src = s_ref.at[pl.ds(first, rows), :, pl.ds(0, cells) if low else pl.ds(CX - cells, cells)]
        return src, pl.ds(EX - 8, cells) if low else pl.ds(8 - cells, cells)

    halo = [
        (always, s_ref.at[pl.ds(1, 3)], u0.at[pl.ds(0, 3), :, mid], (gx, up), always, (0, 1)),
        (always, s_ref.at[pl.ds(0, 3)], u0.at[pl.ds(7, 3), :, mid], (gx, down), always, (2, 1)),
    ]
    for low in (False, True):
        condition, arrives, other, nx = (has_left, from_right, gx - 1, 2) if low else (has_right, from_left, gx + 1, 0)
        src, cells = edge(0, CY, low, HX)
        halo.append((condition, src, u0.at[pl.ds(HY, CY), :, cells], (other, gy), arrives, (1, nx)))
        src, cells = edge(2, 2, low, HX)
        halo.append((condition, src, u0.at[pl.ds(1, 2), :, cells], (other, up), arrives, (0, nx)))
        src, cells = edge(0, 2, low, HX)
        halo.append((condition, src, u0.at[pl.ds(7, 2), :, cells], (other, down), arrives, (2, nx)))
    receipts = []

    def send_halo(i, condition):
        wanted, src, dst, target, arrives, place = halo[i]
        copy = send(wanted & condition, i, src, dst, target)
        small = send(wanted & condition, 8 + i, dd, dn.at[place[0], place[1]], target)
        return [(arrives, copy), (arrives, small)]

    for i in range(len(halo)):
        far = last_z if i in (0, 3, 6) else first_z
        receipts += send_halo(i, always) if i in (2, 5) else send_halo(i, jnp.logical_not(far))
    @pl.when(at_step & (gx != speaker))
    def _():
        pl.semaphore_wait(go_sem, 1)

    for i in (0, 1, 3, 4, 6, 7):
        send_halo(i, last_z if i in (0, 3, 6) else first_z)

    for j in range(SUB):
        @pl.when(is_b)
        def _(j=j):
            arrived(at_rb + j, rb.at[:, pieces[j]])

        for c in range(4):
            row = HY + c
            send(gx == near_fringe[c], at_p + row * SUB + j, rb.at[:, pieces[j]], p0.at[row, :, inner[j]], (zero, gy))
    for j in range(SUB):
        @pl.when(is_b & (gx >= 3) & first_z)
        def _(j=j):
            arrived(at_rbl + j, rbl.at[:, pieces[j]])

        @pl.when(is_b & (gx <= 5) & last_z)
        def _(j=j):
            arrived(at_rbr + j, rbr.at[:, pieces[j]])

        for c in range(4):
            if c >= 1:
                row = c - 1
                send((gx == near_fringe[c]) & first_z, at_p + row * SUB + j, rbl.at[:, pieces[j]], p0.at[row, :, inner[j]], (zero, gy))
            if c <= 2:
                row = 7 + c
                send((gx == near_fringe[c]) & last_z, at_p + row * SUB + j, rbr.at[:, pieces[j]], p0.at[row, :, inner[j]], (zero, gy))

    for j in range(SUB):
        for c in range(4):
            here = p0.at[HY + c, :, inner[j]]

            @pl.when(gx == 0)
            def _(j=j, c=c, here=here):
                arrived(at_p + (HY + c) * SUB + j, here)

            if c >= 1:
                send((gx == 0) & jnp.logical_not(last_z), at_p + (c - 1) * SUB + j, here, p0.at[c - 1, :, inner[j]], (zero, up))
            if c <= 2:
                send((gx == 0) & jnp.logical_not(first_z), at_p + (7 + c) * SUB + j, here, p0.at[7 + c, :, inner[j]], (zero, down))

    @pl.when(gx == 0)
    def _():
        for j in range(SUB):
            for row in (0, 1, 2, 7, 8, 9):
                arrived(at_p + row * SUB + j, p0.at[row, :, inner[j]])

    strip = pl.ds(1, 8)
    for k, (a, b) in enumerate(((64, 0), (8, 8))):
        copy = send(gx == 0, at_strip + k, p0.at[strip, :, pl.ds(a, 8)], p0.at[strip, :, pl.ds(b, 8)], (1 + zero, gy))

        @pl.when(gx == 1)
        def _(copy=copy):
            copy.wait_recv()

    own.wait()
    for condition, copy in receipts:
        @pl.when(condition)
        def _(copy=copy):
            copy.wait_recv()
    for condition, copy in sends:
        @pl.when(condition)
        def _(copy=copy):
            copy.wait_send()

    @pl.when(gx == 0)
    def _():
        @pl.loop(0, ROWS)
        def _(r):
            p0[r, :, 0:8] = p0[r, :, 64:72]
            p0[r, :, 72:80] = p0[r, :, 8:16]
            u0[r, :, 0:8] = p0[r, :, 64:72]

    @pl.when(gx == LAST)
    def _():
        @pl.loop(0, ROWS)
        def _(r):
            u0[r, :, 0:8] = u0[r, :, 64:72]
            u0[r, :, 72:80] = u0[r, :, 8:16]

    lane = lax.broadcasted_iota(jnp.int32, (8, NZ), 1)
    lane_f = lane.astype(jnp.float32)
    sublane = lax.broadcasted_iota(jnp.int32, (8, NZ), 0)

    def disks(place, tile):
        line = dd if place == (1, 1) else dn.at[place[0], place[1]]
        wide = jnp.broadcast_to(line[tile // 2:tile // 2 + 1], (8, NZ))
        value = wide
        for k in range(8):
            shift = 64 * (tile % 2) + 8 * k
            if shift:
                value = jnp.where(sublane == k, pltpu.roll(wide, NZ - shift, 1), value)
        return value

    for ny in range(3):
        rows = {0: (1, 2, 3), 1: (0, 1, 2, 3), 2: (0, 1, 2)}[ny]
        base = {0: -1, 1: 3, 2: 7}[ny]
        for t in range(XT):
            if t == 0:
                spots = jnp.where(from_left, disks((ny, 0), CX // 8 - 1), -1.0)
            elif t == XT - 1:
                spots = jnp.where(from_right, disks((ny, 2), 0), -1.0)
            else:
                spots = disks((ny, 1), t - 1)
            for y in rows:
                one, two = spots[:, 2 * y:2 * y + 1], spots[:, 2 * y + 1:2 * y + 2]
                hit = (lane_f == one) | (lane_f == two)
                thrust[base + y, 8 * t:8 * t + 8] = jnp.where(hit, -0.5 * THRUST_COEFF, 0.0)

    def weights(tile):
        value = jnp.zeros((8, NZ), jnp.float32)
        for k in range(8):
            level = level_ref[8 * tile + k].astype(jnp.float32) / 64.0
            value = jnp.where(sublane == k, level, value)
        return value

    @pl.when(gx == 0)
    def _():
        wt[0:8] = jnp.ones((8, NZ), jnp.float32)
        for t in range(CX // 8):
            wt[8 + 8 * t:16 + 8 * t] = weights(t)

    @pl.when(gx == 1)
    def _():
        wt[0:8] = weights(CX // 8 - 1)

    low_edge, high_edge = lane == 0, lane == NZ - 1

    def terms(which, slot, row, t):
        cells, shifted = pl.ds(8 * t, 8), pl.ds(8 * t + 8, 8)
        u = [st[which, slot, row, f, cells] for f in range(NF)]
        inverse = 1.0 / u[0]
        speed = [u[1] * inverse, u[2] * inverse, u[3] * inverse]
        pressure = 0.4 * (u[4] - 0.5 * (u[1] * speed[0] + u[2] * speed[1] + u[3] * speed[2]))
        total = u[4] + pressure
        flux = []
        for d in range(3):
            part = [u[1 + d], u[1] * speed[d], u[2] * speed[d], u[3] * speed[d], total * speed[d]]
            part[1 + d] = part[1 + d] + pressure
            flux.append(part)
        if which == 0:
            force = thrust[row, cells] * u[1] * jnp.abs(speed[0])
        for f in range(NF):
            ax[row, f, shifted] = u[f] + flux[0][f]
            bx[row, f, shifted] = u[f] - flux[0][f]
            ay[row, f, cells] = u[f] + flux[1][f]
            by[row, f, cells] = u[f] - flux[1][f]
            a, b = u[f] + flux[2][f], u[f] - flux[2][f]
            vertical = jnp.where(low_edge, a, pltpu.roll(a, 1, 1)) + jnp.where(high_edge, b, pltpu.roll(b, NZ - 1, 1))
            rest = 0.5 * vertical - 3.0 * u[f]
            if which == 0 and f == 1:
                rest = rest + force
            if which == 0 and f == 4:
                rest = rest + force * speed[0]
            rr[row, f, cells] = rest

    def edge_terms(which, slot, row, t, sign, ref):
        cells = pl.ds(8 * t, 8)
        u = [st[which, slot, row, f, cells] for f in range(NF)]
        inverse = 1.0 / u[0]
        speed = u[2] * inverse
        square = (u[1] * u[1] + u[2] * u[2] + u[3] * u[3]) * inverse
        pressure = 0.4 * (u[4] - 0.5 * square)
        flux = [u[2], u[1] * speed, u[2] * speed + pressure, u[3] * speed, (u[4] + pressure) * speed]
        for f in range(NF):
            ref[row, f, cells] = u[f] + sign * flux[f]

    def update(which, slot, row, tiles, keep, take):
        for f in range(NF):
            done = []
            for t in range(tiles):
                cells = pl.ds(8 * t, 8)
                near = ax[row, f, pl.ds(8 * t + 7, 8)] + bx[row, f, pl.ds(8 * t + 9, 8)]
                near = near + (ay[row - 1, f, cells] + by[row + 1, f, cells])
                slope = 0.5 * near + rr[row, f, cells]
                fresh = st[which, slot, row, f, cells] + TIME_STEP * slope
                done.append(keep * st[which, 0, row, f, cells] + take * fresh)
            for t in range(tiles):
                st[which, 1, row, f, pl.ds(8 * t, 8)] = done[t]

    def stage(s, carry):
        slot = jnp.minimum(s, 1)
        keep = jnp.where(s == 0, 0.0, jnp.where(s == 1, 0.75, 1.0 / 3.0))
        take = jnp.where(s == 0, 1.0, jnp.where(s == 1, 0.25, 2.0 / 3.0))

        def advance(which, tiles):
            for t in range(tiles):
                edge_terms(which, slot, s, t, 1.0, ay)
            for t in range(tiles):
                edge_terms(which, slot, ROWS - 1 - s, t, -1.0, by)

            @pl.loop(s + 1, ROWS - 1 - s)
            def _(row):
                for t in range(tiles):
                    terms(which, slot, row, t)

            if which == 0:
                @pl.when(gx == LAST - 1)
                def _():
                    @pl.loop(s + 1, ROWS - 1 - s)
                    def _(row):
                        bx[row, :, 80:81] = bx[row, :, 79:80]

            @pl.loop(s + 1, ROWS - 1 - s)
            def _(row):
                update(which, slot, row, tiles, keep, take)

        @pl.when(gx == 0)
        def _():
            advance(1, XT)

        @pl.when(gx == 1)
        def _():
            advance(1, 2)

        advance(0, XT)

        def blend(tiles):
            @pl.loop(s + 1, ROWS - 1 - s)
            def _(row):
                for t in range(tiles):
                    cells = pl.ds(8 * t, 8)
                    weight = wt[cells]
                    for f in range(NF):
                        value = st[0, 1, row, f, cells]
                        st[0, 1, row, f, cells] = value + weight * (st[1, 1, row, f, cells] - value)

        @pl.when(gx == 0)
        def _():
            blend(XT - 1)

        @pl.when(gx == 1)
        def _():
            blend(1)

        return carry

    lax.fori_loop(0, 3, stage, 0)
    for y in range(CY):
        o_ref[y] = st[0, 1, HY + y, :, 8:8 + CX]


def shards(density, velocity, pressure, disk_cells, disk_count, fringe_level):
    with jax.named_scope("state"):
        fields = conserved_from(density, velocity, pressure)
        fields = jnp.transpose(fields, (2, 0, 1, 3))
    cells = disk_cells.reshape(4, NZ)
    vmem = pl.BlockSpec(memory_space=pltpu.VMEM)
    smem = pl.BlockSpec(memory_space=pltpu.SMEM)
    f32 = jnp.float32
    out = pl.pallas_call(
        body,
        out_shape=jax.ShapeDtypeStruct((CY, NF, CX, NZ), f32),
        in_specs=[vmem, vmem, smem, smem],
        out_specs=vmem,
        scratch_shapes=[
            pltpu.VMEM((2, 2, ROWS, NF, EX, NZ), f32),
            pltpu.VMEM((ROWS, NF, EX + 16, NZ), f32),
            pltpu.VMEM((ROWS, NF, EX + 16, NZ), f32),
            pltpu.VMEM((ROWS, NF, EX, NZ), f32),
            pltpu.VMEM((ROWS, NF, EX, NZ), f32),
            pltpu.VMEM((ROWS, NF, EX, NZ), f32),
            pltpu.VMEM((ROWS, EX, NZ), f32),
            pltpu.VMEM((EX, NZ), f32),
            pltpu.VMEM((8, NZ), f32),
            pltpu.VMEM((3, 3, 8, NZ), f32),
            pltpu.VMEM((NF, CX, NZ), f32),
            pltpu.VMEM((NF, CX, NZ), f32),
            pltpu.VMEM((NF, CX, NZ), f32),
            pltpu.VMEM((NF, CX, NZ), f32),
            pltpu.SemaphoreType.REGULAR,
            pltpu.SemaphoreType.DMA,
            pltpu.SemaphoreType.DMA((160,)),
            pltpu.SemaphoreType.DMA((16 + (4 + ROWS) * SUB + 2,)),
        ],
        compiler_params=pltpu.CompilerParams(collective_id=0, has_side_effects=True),
    )(fields, cells, disk_count, fringe_level)
    return jnp.transpose(out, (1, 2, 0, 3))


def solution(mesh):
    in_specs = (
        P("gx", "gy", None),
        P(None, "gx", "gy", None),
        P("gx", "gy", None),
        P("gx", "gy", None),
        P("gx", "gy"),
        P(),
    )
    out_specs = P(None, "gx", "gy", None)
    return jax.shard_map(shards, mesh=mesh, in_specs=in_specs, out_specs=out_specs, check_vma=False)
```

```python
import jax
import jax.numpy as jnp
from jax import lax
from jax.experimental import pallas as pl
from jax.experimental.pallas import tpu as pltpu
from jax.sharding import PartitionSpec as P

TIME_STEP = 0.05
THRUST_COEFF = 0.75
MEAN_WIND = 1.0
MESH = pl.DeviceIdType.MESH

CX, CY, NZ, NF = 64, 4, 128, 5
HY = 3
ROWS = CY + 2 * HY
XT = CX // 8 + 2
EX = 8 * XT
LAST = 15
Z_LO = 16


def conserved_from(density, velocity, pressure):
    stream = velocity[0] + MEAN_WIND
    energy = pressure / 0.4 + 0.5 * density * (
        stream * stream + velocity[1] * velocity[1] + velocity[2] * velocity[2]
    )
    return jnp.stack(
        [density, density * stream, density * velocity[1], density * velocity[2], energy]
    )


HX = 3
SUB = 4
PIECE = CX // SUB


def body(s_ref, d_ref, count_ref, level_ref, o_ref, st, pp, ax, bx, ay, by, rr, thrust, wt, dd, dn, ra, rb, rbl, rbr,
         go_sem, local_sem, send_sem, recv_sem):
    gx, gy = lax.axis_index("gx"), lax.axis_index("gy")
    up, down = lax.rem(gy + 1, 64), lax.rem(gy + 63, 64)
    z_lo = lax.rem(gy, Z_LO)
    first_z, last_z = z_lo == 0, z_lo == Z_LO - 1
    has_right, has_left = gx <= LAST - 2, (gx >= 1) & (gx <= LAST - 1)
    from_left, from_right = (gx >= 1) & (gx <= LAST - 1), gx <= LAST - 2
    u0 = st.at[0]
    p0 = pp.at[0]
    held = (st, pp)
    zero = 0 * gx

    sends = []
    numbers = iter(range(1000))

    def remote(send_index, recv, src, dst, target):
        return pltpu.make_async_remote_copy(
            src_ref=src, dst_ref=dst, send_sem=send_sem.at[send_index], recv_sem=recv_sem.at[recv],
            device_id=target, device_id_type=MESH,
        )

    def send(condition, recv, src, dst, target):
        copy = remote(next(numbers), recv, src, dst, target)
        sends.append((condition, copy))

        @pl.when(condition)
        def _():
            copy.start()

        return copy

    def arrived(recv, dst):
        remote(0, recv, dst, dst, (gx, gy)).wait_recv()

    barrier = pltpu.get_barrier_semaphore()

    def tell(condition, device):
        @pl.when(condition)
        def _():
            pl.semaphore_signal(barrier, inc=1, device_id=device, device_id_type=MESH)

    always = gx >= 0
    is_source = gx == LAST
    near_source = (9, 11, 13, 14)
    near_fringe = (1, 3, 5, 7)
    for c in range(4):
        a, b = near_source[c], near_fringe[c]
        tell(gx == b, (a + zero, gy))
        if c >= 1:
            tell((gx == b) & first_z, (a + zero, down))
        if c <= 2:
            tell((gx == b) & last_z, (a + zero, up))
    at_step = first_z | last_z
    not_first, not_last = jnp.logical_not(first_z), jnp.logical_not(last_z)
    tell(not_last, (gx, up))
    tell(not_first, (gx, down))
    for near, close in ((gy, always), (up, not_last), (down, not_first)):
        tell(from_left & (close | (gx == 8)), (gx - 1, near))
        tell(from_right & (close | (gx == 7)), (gx + 1, near))
    half = jnp.where(gx < 8, 0, 8)
    speaker = jnp.where(gx < 8, 7, 8)
    tell(last_z, (speaker, up))
    tell(first_z, (speaker, down))
    tell(at_step & (gx != speaker), (speaker, gy))
    for c in range(4):
        tell(gx == near_source[c], (LAST + zero, gy))
        tell(gx == 0, (near_fringe[c] + zero, gy))
        if c >= 1:
            tell((gx == 0) & not_first, (near_fringe[c] + zero, down))
        if c <= 2:
            tell((gx == 0) & not_last, (near_fringe[c] + zero, up))

    own = pltpu.make_async_copy(s_ref, u0.at[pl.ds(HY, CY), :, pl.ds(8, CX)], local_sem)
    own.start()

    slot = NZ * lax.broadcasted_iota(jnp.int32, (4, NZ), 0) + lax.broadcasted_iota(jnp.int32, (4, NZ), 1)
    spots = jnp.where(slot < count_ref[0, 0], d_ref[...] & (NZ - 1), -1).astype(jnp.float32)
    dd[0:4] = spots
    dd[4:8] = spots

    def yes(condition):
        return jnp.where(condition, 1, 0)

    is_a = (gx == 9) | (gx == 11) | (gx == 13) | (gx == 14)
    is_b = (gx == 1) | (gx == 3) | (gx == 5) | (gx == 7)
    near_count = 3 - yes(at_step)
    expected = near_count - 1 + 4 * yes(is_source) + yes(is_a) + yes(is_b)
    expected += yes(has_right) * jnp.where(gx == 7, 3, near_count)
    expected += yes(has_left) * jnp.where(gx == 8, 3, near_count)
    expected += 15 * yes(at_step & (gx == speaker))
    expected += yes(is_a & (gx >= 11) & last_z) + yes(is_a & (gx <= 13) & first_z)
    expected += yes(is_b & (gx >= 3) & not_last) + yes(is_b & (gx <= 5) & not_first)
    pl.semaphore_wait(barrier, expected)
    for k in range(8):
        @pl.when(at_step & (gx == speaker) & (gx != half + k))
        def _(k=k):
            pl.semaphore_signal(go_sem, inc=1, device_id=(half + k, gy), device_id_type=MESH)

    at_ra, at_rb, at_rbl, at_rbr, at_p = 16, 16 + SUB, 16 + 2 * SUB, 16 + 3 * SUB, 16 + 4 * SUB
    at_strip = at_p + ROWS * SUB
    pieces = [pl.ds(PIECE * j, PIECE) for j in range(SUB)]
    inner = [pl.ds(8 + PIECE * j, PIECE) for j in range(SUB)]

    for j in range(SUB):
        for c in range(4):
            send(is_source, at_ra + j, s_ref.at[c, :, pieces[j]], ra.at[:, pieces[j]], (near_source[c] + zero, gy))

    @pl.when(is_a)
    def _():
        for j in range(SUB):
            arrived(at_ra + j, ra.at[:, pieces[j]])
    target = gx - 8 + yes(gx == 14)
    for j in range(SUB):
        piece = ra.at[:, pieces[j]]
        send(is_a, at_rb + j, piece, rb.at[:, pieces[j]], (target, gy))
        send(is_a & (gx >= 11) & last_z, at_rbl + j, piece, rbl.at[:, pieces[j]], (target, up))
        send(is_a & (gx <= 13) & first_z, at_rbr + j, piece, rbr.at[:, pieces[j]], (target, down))
    rows_out = sends[4 * SUB:]
    del sends[4 * SUB:]
    for condition, copy in rows_out:
        @pl.when(condition)
        def _(copy=copy):
            copy.wait_send()

    mid = pl.ds(8, CX)
    def edge(first, rows, low, cells):
        src = s_ref.at[pl.ds(first, rows), :, pl.ds(0, cells) if low else pl.ds(CX - cells, cells)]
        return src, pl.ds(EX - 8, cells) if low else pl.ds(8 - cells, cells)

    halo = [
        (always, s_ref.at[pl.ds(1, 3)], u0.at[pl.ds(0, 3), :, mid], (gx, up), always, (0, 1)),
        (always, s_ref.at[pl.ds(0, 3)], u0.at[pl.ds(7, 3), :, mid], (gx, down), always, (2, 1)),
    ]
    for low in (False, True):
        condition, arrives, other, nx = (has_left, from_right, gx - 1, 2) if low else (has_right, from_left, gx + 1, 0)
        src, cells = edge(0, CY, low, HX)
        halo.append((condition, src, u0.at[pl.ds(HY, CY), :, cells], (other, gy), arrives, (1, nx)))
        src, cells = edge(2, 2, low, HX)
        halo.append((condition, src, u0.at[pl.ds(1, 2), :, cells], (other, up), arrives, (0, nx)))
        src, cells = edge(0, 2, low, HX)
        halo.append((condition, src, u0.at[pl.ds(7, 2), :, cells], (other, down), arrives, (2, nx)))
    receipts = []

    def send_halo(i, condition):
        wanted, src, dst, target, arrives, place = halo[i]
        copy = send(wanted & condition, i, src, dst, target)
        small = send(wanted & condition, 8 + i, dd, dn.at[place[0], place[1]], target)
        return [(arrives, copy), (arrives, small)]

    for i in range(len(halo)):
        far = last_z if i in (0, 3, 6) else first_z
        receipts += send_halo(i, always) if i in (2, 5) else send_halo(i, jnp.logical_not(far))
    def send_far(who):
        @pl.when(at_step & (gx != speaker) & who)
        def _():
            pl.semaphore_wait(go_sem, 1)

        for i in (0, 1, 3, 4, 6, 7):
            send_halo(i, (last_z if i in (0, 3, 6) else first_z) & who)

    send_far(always)

    for j in range(SUB):
        @pl.when(is_b)
        def _(j=j):
            arrived(at_rb + j, rb.at[:, pieces[j]])

        for c in range(4):
            row = HY + c
            here, piece = gx == near_fringe[c], rb.at[:, pieces[j]]
            send(here, at_p + row * SUB + j, piece, p0.at[row, :, inner[j]], (zero, gy))
            if c >= 1:
                send(here & not_last, at_p + (c - 1) * SUB + j, piece, p0.at[c - 1, :, inner[j]], (zero, up))
            if c <= 2:
                send(here & not_first, at_p + (7 + c) * SUB + j, piece, p0.at[7 + c, :, inner[j]], (zero, down))
    for j in range(SUB):
        @pl.when(is_b & (gx >= 3) & first_z)
        def _(j=j):
            arrived(at_rbl + j, rbl.at[:, pieces[j]])

        @pl.when(is_b & (gx <= 5) & last_z)
        def _(j=j):
            arrived(at_rbr + j, rbr.at[:, pieces[j]])

        for c in range(4):
            if c >= 1:
                row = c - 1
                send((gx == near_fringe[c]) & first_z, at_p + row * SUB + j, rbl.at[:, pieces[j]], p0.at[row, :, inner[j]], (zero, gy))
            if c <= 2:
                row = 7 + c
                send((gx == near_fringe[c]) & last_z, at_p + row * SUB + j, rbr.at[:, pieces[j]], p0.at[row, :, inner[j]], (zero, gy))

    @pl.when(gx == 0)
    def _():
        for j in range(SUB):
            for row in range(ROWS):
                arrived(at_p + row * SUB + j, p0.at[row, :, inner[j]])

    strip = pl.ds(1, 8)
    for k, (a, b) in enumerate(((64, 0), (8, 8))):
        copy = send(gx == 0, at_strip + k, p0.at[strip, :, pl.ds(a, 8)], p0.at[strip, :, pl.ds(b, 8)], (1 + zero, gy))

        @pl.when(gx == 1)
        def _(copy=copy):
            copy.wait_recv()

    lane = lax.broadcasted_iota(jnp.int32, (8, NZ), 1)
    low_edge, high_edge = lane == 0, lane == NZ - 1

    def terms(which, slot, row, t):
        cells, shifted = pl.ds(8 * t, 8), pl.ds(8 * t + 8, 8)
        u = [held[which][slot, row, f, cells] for f in range(NF)]
        inverse = 1.0 / u[0]
        speed = [u[1] * inverse, u[2] * inverse, u[3] * inverse]
        pressure = 0.4 * (u[4] - 0.5 * (u[1] * speed[0] + u[2] * speed[1] + u[3] * speed[2]))
        total = u[4] + pressure
        flux = []
        for d in range(3):
            part = [u[1 + d], u[1] * speed[d], u[2] * speed[d], u[3] * speed[d], total * speed[d]]
            part[1 + d] = part[1 + d] + pressure
            flux.append(part)
        if which == 0:
            force = thrust[row, cells] * u[1] * jnp.abs(speed[0])
        for f in range(NF):
            ax[row, f, shifted] = u[f] + flux[0][f]
            bx[row, f, shifted] = u[f] - flux[0][f]
            ay[row, f, cells] = u[f] + flux[1][f]
            by[row, f, cells] = u[f] - flux[1][f]
            a, b = u[f] + flux[2][f], u[f] - flux[2][f]
            vertical = jnp.where(low_edge, a, pltpu.roll(a, 1, 1)) + jnp.where(high_edge, b, pltpu.roll(b, NZ - 1, 1))
            rest = 0.5 * vertical - 3.0 * u[f]
            if which == 0 and f == 1:
                rest = rest + force
            if which == 0 and f == 4:
                rest = rest + force * speed[0]
            rr[row, f, cells] = rest

    def edge_terms(which, slot, row, t, sign, ref):
        cells = pl.ds(8 * t, 8)
        u = [held[which][slot, row, f, cells] for f in range(NF)]
        inverse = 1.0 / u[0]
        speed = u[2] * inverse
        square = (u[1] * u[1] + u[2] * u[2] + u[3] * u[3]) * inverse
        pressure = 0.4 * (u[4] - 0.5 * square)
        flux = [u[2], u[1] * speed, u[2] * speed + pressure, u[3] * speed, (u[4] + pressure) * speed]
        for f in range(NF):
            ref[row, f, cells] = u[f] + sign * flux[f]

    def update(which, slot, out, row, tiles, keep, take):
        for f in range(NF):
            done = []
            for t in range(tiles):
                cells = pl.ds(8 * t, 8)
                near = ax[row, f, pl.ds(8 * t + 7, 8)] + bx[row, f, pl.ds(8 * t + 9, 8)]
                near = near + (ay[row - 1, f, cells] + by[row + 1, f, cells])
                slope = 0.5 * near + rr[row, f, cells]
                fresh = held[which][slot, row, f, cells] + TIME_STEP * slope
                done.append(keep * held[which][0, row, f, cells] + take * fresh)
            for t in range(tiles):
                held[which][out, row, f, pl.ds(8 * t, 8)] = done[t]

    def advance(s, which, slot, out, tiles):
        keep = jnp.where(s == 0, 0.0, jnp.where(s == 1, 0.75, 1.0 / 3.0))
        take = jnp.where(s == 0, 1.0, jnp.where(s == 1, 0.25, 2.0 / 3.0))

        for t in range(tiles):
            edge_terms(which, slot, s, t, 1.0, ay)
        for t in range(tiles):
            edge_terms(which, slot, ROWS - 1 - s, t, -1.0, by)

        @pl.loop(s + 1, ROWS - 1 - s)
        def _(row):
            for t in range(tiles):
                terms(which, slot, row, t)

        if which == 0:
            @pl.when(gx == LAST - 1)
            def _():
                @pl.loop(s + 1, ROWS - 1 - s)
                def _(row):
                    bx[row, :, 80:81] = bx[row, :, 79:80]

        @pl.loop(s + 1, ROWS - 1 - s)
        def _(row):
            update(which, slot, out, row, tiles, keep, take)

    def precursor(tiles):
        def one(s, carry):
            advance(s, 1, s, s + 1, tiles)
            return carry

        lax.fori_loop(0, 3, one, 0)

    @pl.when(gx == 0)
    def _():
        @pl.loop(0, ROWS)
        def _(r):
            p0[r, :, 0:8] = p0[r, :, 64:72]
            p0[r, :, 72:80] = p0[r, :, 8:16]

        precursor(XT)

    @pl.when(gx == 1)
    def _():
        precursor(2)

    own.wait()
    for condition, copy in receipts:
        @pl.when(condition)
        def _(copy=copy):
            copy.wait_recv()
    for condition, copy in sends:
        @pl.when(condition)
        def _(copy=copy):
            copy.wait_send()

    @pl.when(gx == 0)
    def _():
        @pl.loop(0, ROWS)
        def _(r):
            u0[r, :, 0:8] = p0[r, :, 64:72]

    @pl.when(gx == LAST)
    def _():
        @pl.loop(0, ROWS)
        def _(r):
            u0[r, :, 0:8] = u0[r, :, 64:72]
            u0[r, :, 72:80] = u0[r, :, 8:16]

    lane_f = lane.astype(jnp.float32)
    sublane = lax.broadcasted_iota(jnp.int32, (8, NZ), 0)

    def disks(place, tile):
        line = dd if place == (1, 1) else dn.at[place[0], place[1]]
        wide = jnp.broadcast_to(line[tile // 2:tile // 2 + 1], (8, NZ))
        value = wide
        for k in range(8):
            shift = 64 * (tile % 2) + 8 * k
            if shift:
                value = jnp.where(sublane == k, pltpu.roll(wide, NZ - shift, 1), value)
        return value

    for ny in range(3):
        rows = {0: (1, 2, 3), 1: (0, 1, 2, 3), 2: (0, 1, 2)}[ny]
        base = {0: -1, 1: 3, 2: 7}[ny]
        for t in range(XT):
            if t == 0:
                spots = jnp.where(from_left, disks((ny, 0), CX // 8 - 1), -1.0)
            elif t == XT - 1:
                spots = jnp.where(from_right, disks((ny, 2), 0), -1.0)
            else:
                spots = disks((ny, 1), t - 1)
            for y in rows:
                one, two = spots[:, 2 * y:2 * y + 1], spots[:, 2 * y + 1:2 * y + 2]
                hit = (lane_f == one) | (lane_f == two)
                thrust[base + y, 8 * t:8 * t + 8] = jnp.where(hit, -0.5 * THRUST_COEFF, 0.0)

    def weights(tile):
        value = jnp.zeros((8, NZ), jnp.float32)
        for k in range(8):
            level = level_ref[8 * tile + k].astype(jnp.float32) / 64.0
            value = jnp.where(sublane == k, level, value)
        return value

    @pl.when(gx == 0)
    def _():
        wt[0:8] = jnp.ones((8, NZ), jnp.float32)
        for t in range(CX // 8):
            wt[8 + 8 * t:16 + 8 * t] = weights(t)

    @pl.when(gx == 1)
    def _():
        wt[0:8] = weights(CX // 8 - 1)

    def stage(s, carry):
        advance(s, 0, jnp.minimum(s, 1), 1, XT)

        def blend(tiles):
            @pl.loop(s + 1, ROWS - 1 - s)
            def _(row):
                for t in range(tiles):
                    cells = pl.ds(8 * t, 8)
                    weight = wt[cells]
                    for f in range(NF):
                        value = st[1, row, f, cells]
                        st[1, row, f, cells] = value + weight * (pp[s + 1, row, f, cells] - value)

        @pl.when(gx == 0)
        def _():
            blend(XT - 1)

        @pl.when(gx == 1)
        def _():
            blend(1)

        return carry

    lax.fori_loop(0, 3, stage, 0)
    for y in range(CY):
        o_ref[y] = st[1, HY + y, :, 8:8 + CX]


def shards(density, velocity, pressure, disk_cells, disk_count, fringe_level):
    with jax.named_scope("state"):
        fields = conserved_from(density, velocity, pressure)
        fields = jnp.transpose(fields, (2, 0, 1, 3))
    cells = disk_cells.reshape(4, NZ)
    vmem = pl.BlockSpec(memory_space=pltpu.VMEM)
    smem = pl.BlockSpec(memory_space=pltpu.SMEM)
    f32 = jnp.float32
    out = pl.pallas_call(
        body,
        out_shape=jax.ShapeDtypeStruct((CY, NF, CX, NZ), f32),
        in_specs=[vmem, vmem, smem, smem],
        out_specs=vmem,
        scratch_shapes=[
            pltpu.VMEM((2, ROWS, NF, EX, NZ), f32),
            pltpu.VMEM((4, ROWS, NF, EX, NZ), f32),
            pltpu.VMEM((ROWS, NF, EX + 16, NZ), f32),
            pltpu.VMEM((ROWS, NF, EX + 16, NZ), f32),
            pltpu.VMEM((ROWS, NF, EX, NZ), f32),
            pltpu.VMEM((ROWS, NF, EX, NZ), f32),
            pltpu.VMEM((ROWS, NF, EX, NZ), f32),
            pltpu.VMEM((ROWS, EX, NZ), f32),
            pltpu.VMEM((EX, NZ), f32),
            pltpu.VMEM((8, NZ), f32),
            pltpu.VMEM((3, 3, 8, NZ), f32),
            pltpu.VMEM((NF, CX, NZ), f32),
            pltpu.VMEM((NF, CX, NZ), f32),
            pltpu.VMEM((NF, CX, NZ), f32),
            pltpu.VMEM((NF, CX, NZ), f32),
            pltpu.SemaphoreType.REGULAR,
            pltpu.SemaphoreType.DMA,
            pltpu.SemaphoreType.DMA((220,)),
            pltpu.SemaphoreType.DMA((16 + (4 + ROWS) * SUB + 2,)),
        ],
        compiler_params=pltpu.CompilerParams(collective_id=0, has_side_effects=True),
    )(fields, cells, disk_count, fringe_level)
    return jnp.transpose(out, (1, 2, 0, 3))


def solution(mesh):
    in_specs = (
        P("gx", "gy", None),
        P(None, "gx", "gy", None),
        P("gx", "gy", None),
        P("gx", "gy", None),
        P("gx", "gy"),
        P(),
    )
    out_specs = P(None, "gx", "gy", None)
    return jax.shard_map(shards, mesh=mesh, in_specs=in_specs, out_specs=out_specs, check_vma=False)
```

```python
import jax
import jax.numpy as jnp
from jax import lax
from jax.experimental import pallas as pl
from jax.experimental.pallas import tpu as pltpu
from jax.sharding import PartitionSpec as P

TIME_STEP = 0.05
THRUST_COEFF = 0.75
MEAN_WIND = 1.0
MESH = pl.DeviceIdType.MESH

CX, CY, NZ, NF = 64, 4, 128, 5
HY = 3
ROWS = CY + 2 * HY
XT = CX // 8 + 2
EX = 8 * XT
LAST = 15
Z_LO = 16


def conserved_from(density, velocity, pressure):
    stream = velocity[0] + MEAN_WIND
    energy = pressure / 0.4 + 0.5 * density * (
        stream * stream + velocity[1] * velocity[1] + velocity[2] * velocity[2]
    )
    return jnp.stack(
        [density, density * stream, density * velocity[1], density * velocity[2], energy]
    )


HX = 3
SUB = 4
PIECE = CX // SUB


def body(s_ref, d_ref, count_ref, level_ref, o_ref, st, pp, ax, bx, ay, by, rr, thrust, wt, dd, dn, ra, rb, rbl, rbr,
         go_sem, local_sem, send_sem, recv_sem):
    gx, gy = lax.axis_index("gx"), lax.axis_index("gy")
    up, down = lax.rem(gy + 1, 64), lax.rem(gy + 63, 64)
    z_lo = lax.rem(gy, Z_LO)
    first_z, last_z = z_lo == 0, z_lo == Z_LO - 1
    has_right, has_left = gx <= LAST - 2, (gx >= 1) & (gx <= LAST - 1)
    from_left, from_right = (gx >= 1) & (gx <= LAST - 1), gx <= LAST - 2
    u0 = st.at[0]
    p0 = pp.at[0]
    held = (st, pp)
    zero = 0 * gx

    sends = []
    numbers = iter(range(1000))

    def remote(send_index, recv, src, dst, target):
        return pltpu.make_async_remote_copy(
            src_ref=src, dst_ref=dst, send_sem=send_sem.at[send_index], recv_sem=recv_sem.at[recv],
            device_id=target, device_id_type=MESH,
        )

    def send(condition, recv, src, dst, target):
        copy = remote(next(numbers), recv, src, dst, target)
        sends.append((condition, copy))

        @pl.when(condition)
        def _():
            copy.start()

        return copy

    def arrived(recv, dst):
        remote(0, recv, dst, dst, (gx, gy)).wait_recv()

    barrier = pltpu.get_barrier_semaphore()

    def tell(condition, device):
        @pl.when(condition)
        def _():
            pl.semaphore_signal(barrier, inc=1, device_id=device, device_id_type=MESH)

    always = gx >= 0
    is_source = gx == LAST
    near_source = (9, 11, 13, 14)
    near_fringe = (1, 3, 5, 7)
    for c in range(4):
        a, b = near_source[c], near_fringe[c]
        tell(gx == b, (a + zero, gy))
        if c >= 1:
            tell((gx == b) & first_z, (a + zero, down))
        if c <= 2:
            tell((gx == b) & last_z, (a + zero, up))
    at_step = first_z | last_z
    not_first, not_last = jnp.logical_not(first_z), jnp.logical_not(last_z)
    tell(not_last, (gx, up))
    tell(not_first, (gx, down))
    for near, close in ((gy, always), (up, not_last), (down, not_first)):
        tell(from_left & (close | (gx == 8)), (gx - 1, near))
        tell(from_right & (close | (gx == 7)), (gx + 1, near))
    half = jnp.where(gx < 8, 0, 8)
    speaker = jnp.where(gx < 8, 7, 8)
    tell(last_z, (speaker, up))
    tell(first_z, (speaker, down))
    tell(at_step & (gx != speaker), (speaker, gy))
    for c in range(4):
        tell(gx == near_source[c], (LAST + zero, gy))
        tell(gx == 0, (near_fringe[c] + zero, gy))
        if c >= 1:
            tell((gx == 0) & not_first, (near_fringe[c] + zero, down))
        if c <= 2:
            tell((gx == 0) & not_last, (near_fringe[c] + zero, up))

    own = pltpu.make_async_copy(s_ref, u0.at[pl.ds(HY, CY), :, pl.ds(8, CX)], local_sem)
    own.start()

    slot = NZ * lax.broadcasted_iota(jnp.int32, (4, NZ), 0) + lax.broadcasted_iota(jnp.int32, (4, NZ), 1)
    spots = jnp.where(slot < count_ref[0, 0], d_ref[...] & (NZ - 1), -1).astype(jnp.float32)
    dd[0:4] = spots
    dd[4:8] = spots

    def yes(condition):
        return jnp.where(condition, 1, 0)

    is_a = (gx == 9) | (gx == 11) | (gx == 13) | (gx == 14)
    is_b = (gx == 1) | (gx == 3) | (gx == 5) | (gx == 7)
    near_count = 3 - yes(at_step)
    expected = near_count - 1 + 4 * yes(is_source) + yes(is_a) + yes(is_b)
    expected += yes(has_right) * jnp.where(gx == 7, 3, near_count)
    expected += yes(has_left) * jnp.where(gx == 8, 3, near_count)
    expected += 15 * yes(at_step & (gx == speaker))
    expected += yes(is_a & (gx >= 11) & last_z) + yes(is_a & (gx <= 13) & first_z)
    expected += yes(is_b & (gx >= 3) & not_last) + yes(is_b & (gx <= 5) & not_first)
    pl.semaphore_wait(barrier, expected)
    for k in range(8):
        @pl.when(at_step & (gx == speaker) & (gx != half + k))
        def _(k=k):
            pl.semaphore_signal(go_sem, inc=1, device_id=(half + k, gy), device_id_type=MESH)

    at_ra, at_rb, at_rbl, at_rbr, at_p = 16, 16 + SUB, 16 + 2 * SUB, 16 + 3 * SUB, 16 + 4 * SUB
    at_strip = at_p + ROWS * SUB
    pieces = [pl.ds(PIECE * j, PIECE) for j in range(SUB)]
    inner = [pl.ds(8 + PIECE * j, PIECE) for j in range(SUB)]

    for j in range(SUB):
        for c in range(4):
            send(is_source, at_ra + j, s_ref.at[c, :, pieces[j]], ra.at[:, pieces[j]], (near_source[c] + zero, gy))

    @pl.when(is_a)
    def _():
        for j in range(SUB):
            arrived(at_ra + j, ra.at[:, pieces[j]])
    target = gx - 8 + yes(gx == 14)
    for j in range(SUB):
        piece = ra.at[:, pieces[j]]
        send(is_a, at_rb + j, piece, rb.at[:, pieces[j]], (target, gy))
        send(is_a & (gx >= 11) & last_z, at_rbl + j, piece, rbl.at[:, pieces[j]], (target, up))
        send(is_a & (gx <= 13) & first_z, at_rbr + j, piece, rbr.at[:, pieces[j]], (target, down))
    rows_out = sends[4 * SUB:]
    del sends[4 * SUB:]
    for condition, copy in rows_out:
        @pl.when(condition)
        def _(copy=copy):
            copy.wait_send()

    mid = pl.ds(8, CX)
    def edge(first, rows, low, cells):
        src = s_ref.at[pl.ds(first, rows), :, pl.ds(0, cells) if low else pl.ds(CX - cells, cells)]
        return src, pl.ds(EX - 8, cells) if low else pl.ds(8 - cells, cells)

    halo = [
        (always, s_ref.at[pl.ds(1, 3)], u0.at[pl.ds(0, 3), :, mid], (gx, up), always, (0, 1)),
        (always, s_ref.at[pl.ds(0, 3)], u0.at[pl.ds(7, 3), :, mid], (gx, down), always, (2, 1)),
    ]
    for low in (False, True):
        condition, arrives, other, nx = (has_left, from_right, gx - 1, 2) if low else (has_right, from_left, gx + 1, 0)
        src, cells = edge(0, CY, low, HX)
        halo.append((condition, src, u0.at[pl.ds(HY, CY), :, cells], (other, gy), arrives, (1, nx)))
        src, cells = edge(2, 2, low, HX)
        halo.append((condition, src, u0.at[pl.ds(1, 2), :, cells], (other, up), arrives, (0, nx)))
        src, cells = edge(0, 2, low, HX)
        halo.append((condition, src, u0.at[pl.ds(7, 2), :, cells], (other, down), arrives, (2, nx)))
    receipts = []

    def send_halo(i, condition):
        wanted, src, dst, target, arrives, place = halo[i]
        copy = send(wanted & condition, i, src, dst, target)
        small = send(wanted & condition, 8 + i, dd, dn.at[place[0], place[1]], target)
        return [(arrives, copy), (arrives, small)]

    for i in range(len(halo)):
        far = last_z if i in (0, 3, 6) else first_z
        receipts += send_halo(i, always) if i in (2, 5) else send_halo(i, jnp.logical_not(far))
    def send_far(who):
        @pl.when(at_step & (gx != speaker) & who)
        def _():
            pl.semaphore_wait(go_sem, 1)

        for i in (0, 1, 3, 4, 6, 7):
            send_halo(i, (last_z if i in (0, 3, 6) else first_z) & who)

    send_far(always)

    for j in range(SUB):
        @pl.when(is_b)
        def _(j=j):
            arrived(at_rb + j, rb.at[:, pieces[j]])

        for c in range(4):
            row = HY + c
            here, piece = gx == near_fringe[c], rb.at[:, pieces[j]]
            send(here, at_p + row * SUB + j, piece, p0.at[row, :, inner[j]], (zero, gy))
            if c >= 1:
                send(here & not_last, at_p + (c - 1) * SUB + j, piece, p0.at[c - 1, :, inner[j]], (zero, up))
            if c <= 2:
                send(here & not_first, at_p + (7 + c) * SUB + j, piece, p0.at[7 + c, :, inner[j]], (zero, down))
    for j in range(SUB):
        @pl.when(is_b & (gx >= 3) & first_z)
        def _(j=j):
            arrived(at_rbl + j, rbl.at[:, pieces[j]])

        @pl.when(is_b & (gx <= 5) & last_z)
        def _(j=j):
            arrived(at_rbr + j, rbr.at[:, pieces[j]])

        for c in range(4):
            if c >= 1:
                row = c - 1
                send((gx == near_fringe[c]) & first_z, at_p + row * SUB + j, rbl.at[:, pieces[j]], p0.at[row, :, inner[j]], (zero, gy))
            if c <= 2:
                row = 7 + c
                send((gx == near_fringe[c]) & last_z, at_p + row * SUB + j, rbr.at[:, pieces[j]], p0.at[row, :, inner[j]], (zero, gy))

    @pl.when(gx == 0)
    def _():
        for j in range(SUB):
            for row in range(ROWS):
                arrived(at_p + row * SUB + j, p0.at[row, :, inner[j]])

    strip = pl.ds(1, 8)
    for k, (a, b) in enumerate(((64, 0), (8, 8))):
        copy = send(gx == 0, at_strip + k, p0.at[strip, :, pl.ds(a, 8)], p0.at[strip, :, pl.ds(b, 8)], (1 + zero, gy))

        @pl.when(gx == 1)
        def _(copy=copy):
            copy.wait_recv()

    lane = lax.broadcasted_iota(jnp.int32, (8, NZ), 1)
    low_edge, high_edge = lane == 0, lane == NZ - 1

    def terms(which, slot, row, t):
        cells, shifted = pl.ds(8 * t, 8), pl.ds(8 * t + 8, 8)
        u = [held[which][slot, row, f, cells] for f in range(NF)]
        inverse = 1.0 / u[0]
        speed = [u[1] * inverse, u[2] * inverse, u[3] * inverse]
        pressure = 0.4 * (u[4] - 0.5 * (u[1] * speed[0] + u[2] * speed[1] + u[3] * speed[2]))
        total = u[4] + pressure
        flux = []
        for d in range(3):
            part = [u[1 + d], u[1] * speed[d], u[2] * speed[d], u[3] * speed[d], total * speed[d]]
            part[1 + d] = part[1 + d] + pressure
            flux.append(part)
        if which == 0:
            force = thrust[row, cells] * u[1] * jnp.abs(speed[0])
        for f in range(NF):
            ax[row, f, shifted] = u[f] + flux[0][f]
            bx[row, f, shifted] = u[f] - flux[0][f]
            ay[row, f, cells] = u[f] + flux[1][f]
            by[row, f, cells] = u[f] - flux[1][f]
            a, b = u[f] + flux[2][f], u[f] - flux[2][f]
            vertical = jnp.where(low_edge, a, pltpu.roll(a, 1, 1)) + jnp.where(high_edge, b, pltpu.roll(b, NZ - 1, 1))
            rest = 0.5 * vertical - 3.0 * u[f]
            if which == 0 and f == 1:
                rest = rest + force
            if which == 0 and f == 4:
                rest = rest + force * speed[0]
            rr[row, f, cells] = rest

    def edge_terms(which, slot, row, t, sign, ref):
        cells = pl.ds(8 * t, 8)
        u = [held[which][slot, row, f, cells] for f in range(NF)]
        inverse = 1.0 / u[0]
        speed = u[2] * inverse
        square = (u[1] * u[1] + u[2] * u[2] + u[3] * u[3]) * inverse
        pressure = 0.4 * (u[4] - 0.5 * square)
        flux = [u[2], u[1] * speed, u[2] * speed + pressure, u[3] * speed, (u[4] + pressure) * speed]
        for f in range(NF):
            ref[row, f, cells] = u[f] + sign * flux[f]

    def update(which, slot, out, row, tiles, keep, take):
        for f in range(NF):
            done = []
            for t in range(tiles):
                cells = pl.ds(8 * t, 8)
                near = ax[row, f, pl.ds(8 * t + 7, 8)] + bx[row, f, pl.ds(8 * t + 9, 8)]
                near = near + (ay[row - 1, f, cells] + by[row + 1, f, cells])
                slope = 0.5 * near + rr[row, f, cells]
                fresh = held[which][slot, row, f, cells] + TIME_STEP * slope
                done.append(keep * held[which][0, row, f, cells] + take * fresh)
            for t in range(tiles):
                held[which][out, row, f, pl.ds(8 * t, 8)] = done[t]

    def advance(s, which, slot, out, tiles):
        keep = jnp.where(s == 0, 0.0, jnp.where(s == 1, 0.75, 1.0 / 3.0))
        take = jnp.where(s == 0, 1.0, jnp.where(s == 1, 0.25, 2.0 / 3.0))

        for t in range(tiles):
            edge_terms(which, slot, s, t, 1.0, ay)
        for t in range(tiles):
            edge_terms(which, slot, ROWS - 1 - s, t, -1.0, by)

        @pl.loop(s + 1, ROWS - 1 - s)
        def _(row):
            for t in range(tiles):
                terms(which, slot, row, t)

        if which == 0:
            @pl.when(gx == LAST - 1)
            def _():
                @pl.loop(s + 1, ROWS - 1 - s)
                def _(row):
                    bx[row, :, 80:81] = bx[row, :, 79:80]

        @pl.loop(s + 1, ROWS - 1 - s)
        def _(row):
            update(which, slot, out, row, tiles, keep, take)

    def precursor(tiles):
        def one(s, carry):
            advance(s, 1, s, s + 1, tiles)
            return carry

        lax.fori_loop(0, 3, one, 0)

    @pl.when(gx == 0)
    def _():
        @pl.loop(0, ROWS)
        def _(r):
            p0[r, :, 0:8] = p0[r, :, 64:72]
            p0[r, :, 72:80] = p0[r, :, 8:16]

        precursor(XT)

    @pl.when(gx == 1)
    def _():
        precursor(2)

    own.wait()
    for condition, copy in receipts:
        @pl.when(condition)
        def _(copy=copy):
            copy.wait_recv()
    for condition, copy in sends:
        @pl.when(condition)
        def _(copy=copy):
            copy.wait_send()

    @pl.when(gx == 0)
    def _():
        @pl.loop(0, ROWS)
        def _(r):
            u0[r, :, 0:8] = p0[r, :, 64:72]

    @pl.when(gx == LAST)
    def _():
        @pl.loop(0, ROWS)
        def _(r):
            u0[r, :, 0:8] = u0[r, :, 64:72]
            u0[r, :, 72:80] = u0[r, :, 8:16]

    lane_f = lane.astype(jnp.float32)
    sublane = lax.broadcasted_iota(jnp.int32, (8, NZ), 0)

    def disks(place, tile):
        line = dd if place == (1, 1) else dn.at[place[0], place[1]]
        wide = jnp.broadcast_to(line[tile // 2:tile // 2 + 1], (8, NZ))
        value = wide
        for k in range(8):
            shift = 64 * (tile % 2) + 8 * k
            if shift:
                value = jnp.where(sublane == k, pltpu.roll(wide, NZ - shift, 1), value)
        return value

    for ny in range(3):
        rows = {0: (1, 2, 3), 1: (0, 1, 2, 3), 2: (0, 1, 2)}[ny]
        base = {0: -1, 1: 3, 2: 7}[ny]
        for t in range(XT):
            if t == 0:
                spots = jnp.where(from_left, disks((ny, 0), CX // 8 - 1), -1.0)
            elif t == XT - 1:
                spots = jnp.where(from_right, disks((ny, 2), 0), -1.0)
            else:
                spots = disks((ny, 1), t - 1)
            for y in rows:
                one, two = spots[:, 2 * y:2 * y + 1], spots[:, 2 * y + 1:2 * y + 2]
                hit = (lane_f == one) | (lane_f == two)
                thrust[base + y, 8 * t:8 * t + 8] = jnp.where(hit, -0.5 * THRUST_COEFF, 0.0)

    def weights(tile):
        value = jnp.zeros((8, NZ), jnp.float32)
        for k in range(8):
            level = level_ref[8 * tile + k].astype(jnp.float32) / 64.0
            value = jnp.where(sublane == k, level, value)
        return value

    @pl.when(gx == 0)
    def _():
        wt[0:8] = jnp.ones((8, NZ), jnp.float32)
        for t in range(CX // 8):
            wt[8 + 8 * t:16 + 8 * t] = weights(t)

    @pl.when(gx == 1)
    def _():
        wt[0:8] = weights(CX // 8 - 1)

    def stage(s, carry):
        advance(s, 0, jnp.minimum(s, 1), 1, XT)

        def blend(tiles):
            @pl.loop(s + 1, ROWS - 1 - s)
            def _(row):
                for t in range(tiles):
                    cells = pl.ds(8 * t, 8)
                    weight = wt[cells]
                    for f in range(NF):
                        value = st[1, row, f, cells]
                        st[1, row, f, cells] = value + weight * (pp[s + 1, row, f, cells] - value)

        @pl.when(gx == 0)
        def _():
            blend(XT - 1)

        @pl.when(gx == 1)
        def _():
            blend(1)

        return carry

    lax.fori_loop(0, 3, stage, 0)
    for y in range(CY):
        o_ref[:, y] = st[1, HY + y, :, 8:8 + CX]


def shards(density, velocity, pressure, disk_cells, disk_count, fringe_level):
    with jax.named_scope("state"):
        fields = conserved_from(density, velocity, pressure)
        fields = jnp.transpose(fields, (2, 0, 1, 3))
    cells = disk_cells.reshape(4, NZ)
    vmem = pl.BlockSpec(memory_space=pltpu.VMEM)
    smem = pl.BlockSpec(memory_space=pltpu.SMEM)
    f32 = jnp.float32
    out = pl.pallas_call(
        body,
        out_shape=jax.ShapeDtypeStruct((NF, CY, CX, NZ), f32),
        in_specs=[vmem, vmem, smem, smem],
        out_specs=vmem,
        scratch_shapes=[
            pltpu.VMEM((2, ROWS, NF, EX, NZ), f32),
            pltpu.VMEM((4, ROWS, NF, EX, NZ), f32),
            pltpu.VMEM((ROWS, NF, EX + 16, NZ), f32),
            pltpu.VMEM((ROWS, NF, EX + 16, NZ), f32),
            pltpu.VMEM((ROWS, NF, EX, NZ), f32),
            pltpu.VMEM((ROWS, NF, EX, NZ), f32),
            pltpu.VMEM((ROWS, NF, EX, NZ), f32),
            pltpu.VMEM((ROWS, EX, NZ), f32),
            pltpu.VMEM((EX, NZ), f32),
            pltpu.VMEM((8, NZ), f32),
            pltpu.VMEM((3, 3, 8, NZ), f32),
            pltpu.VMEM((NF, CX, NZ), f32),
            pltpu.VMEM((NF, CX, NZ), f32),
            pltpu.VMEM((NF, CX, NZ), f32),
            pltpu.VMEM((NF, CX, NZ), f32),
            pltpu.SemaphoreType.REGULAR,
            pltpu.SemaphoreType.DMA,
            pltpu.SemaphoreType.DMA((220,)),
            pltpu.SemaphoreType.DMA((16 + (4 + ROWS) * SUB + 2,)),
        ],
        compiler_params=pltpu.CompilerParams(collective_id=0, has_side_effects=True),
    )(fields, cells, disk_count, fringe_level)
    return jnp.transpose(out, (0, 2, 1, 3))


def solution(mesh):
    in_specs = (
        P("gx", "gy", None),
        P(None, "gx", "gy", None),
        P("gx", "gy", None),
        P("gx", "gy", None),
        P("gx", "gy"),
        P(),
    )
    out_specs = P(None, "gx", "gy", None)
    return jax.shard_map(shards, mesh=mesh, in_specs=in_specs, out_specs=out_specs, check_vma=False)
```

```python
import jax
import jax.numpy as jnp
from jax import lax
from jax.experimental import pallas as pl
from jax.experimental.pallas import tpu as pltpu
from jax.sharding import PartitionSpec as P

TIME_STEP = 0.05
THRUST_COEFF = 0.75
MEAN_WIND = 1.0
MESH = pl.DeviceIdType.MESH

CX, CY, NZ, NF = 64, 4, 128, 5
HY = 3
ROWS = CY + 2 * HY
XT = CX // 8 + 2
EX = 8 * XT
LAST = 15
Z_LO = 16


def conserved_from(density, velocity, pressure):
    stream = velocity[0] + MEAN_WIND
    energy = pressure / 0.4 + 0.5 * density * (
        stream * stream + velocity[1] * velocity[1] + velocity[2] * velocity[2]
    )
    return jnp.stack(
        [density, density * stream, density * velocity[1], density * velocity[2], energy]
    )


HX = 3
SUB = 4
PIECE = CX // SUB


def body(s_ref, d_ref, count_ref, level_ref, o_ref, st, pp, ax, bx, ay, by, rr, thrust, wt, dd, dn, ra, rb, rbl, rbr,
         go_sem, local_sem, send_sem, recv_sem):
    gx, gy = lax.axis_index("gx"), lax.axis_index("gy")
    up, down = lax.rem(gy + 1, 64), lax.rem(gy + 63, 64)
    z_lo = lax.rem(gy, Z_LO)
    first_z, last_z = z_lo == 0, z_lo == Z_LO - 1
    has_right, has_left = gx <= LAST - 2, (gx >= 1) & (gx <= LAST - 1)
    from_left, from_right = (gx >= 1) & (gx <= LAST - 1), gx <= LAST - 2
    u0 = st.at[0]
    p0 = pp.at[0]
    held = (st, pp)
    zero = 0 * gx

    sends = []
    numbers = iter(range(1000))

    def remote(send_index, recv, src, dst, target):
        return pltpu.make_async_remote_copy(
            src_ref=src, dst_ref=dst, send_sem=send_sem.at[send_index], recv_sem=recv_sem.at[recv],
            device_id=target, device_id_type=MESH,
        )

    def send(condition, recv, src, dst, target):
        copy = remote(next(numbers), recv, src, dst, target)
        sends.append((condition, copy))

        @pl.when(condition)
        def _():
            copy.start()

        return copy

    def arrived(recv, dst):
        remote(0, recv, dst, dst, (gx, gy)).wait_recv()

    barrier = pltpu.get_barrier_semaphore()

    def tell(condition, device):
        @pl.when(condition)
        def _():
            pl.semaphore_signal(barrier, inc=1, device_id=device, device_id_type=MESH)

    always = gx >= 0
    is_source = gx == LAST
    near_source = (9, 11, 13, 14)
    near_fringe = (1, 3, 5, 7)
    for c in range(4):
        a, b = near_source[c], near_fringe[c]
        tell(gx == b, (a + zero, gy))
        if c >= 1:
            tell((gx == b) & first_z, (a + zero, down))
        if c <= 2:
            tell((gx == b) & last_z, (a + zero, up))
    at_step = first_z | last_z
    not_first, not_last = jnp.logical_not(first_z), jnp.logical_not(last_z)
    tell(not_last, (gx, up))
    tell(not_first, (gx, down))
    for near, close in ((gy, always), (up, not_last), (down, not_first)):
        tell(from_left & (close | (gx == 8)), (gx - 1, near))
        tell(from_right & (close | (gx == 7)), (gx + 1, near))
    half = jnp.where(gx < 8, 0, 8)
    speaker = jnp.where(gx < 8, 7, 8)
    tell(last_z, (speaker, up))
    tell(first_z, (speaker, down))
    tell(at_step & (gx != speaker), (speaker, gy))
    for c in range(4):
        tell(gx == near_source[c], (LAST + zero, gy))
        tell(gx == 0, (near_fringe[c] + zero, gy))
        if c >= 1:
            tell((gx == 0) & not_first, (near_fringe[c] + zero, down))
        if c <= 2:
            tell((gx == 0) & not_last, (near_fringe[c] + zero, up))

    own = pltpu.make_async_copy(s_ref, u0.at[pl.ds(HY, CY), :, pl.ds(8, CX)], local_sem)
    own.start()

    slot = NZ * lax.broadcasted_iota(jnp.int32, (4, NZ), 0) + lax.broadcasted_iota(jnp.int32, (4, NZ), 1)
    spots = jnp.where(slot < count_ref[0, 0], d_ref[...] & (NZ - 1), -1).astype(jnp.float32)
    dd[0:4] = spots
    dd[4:8] = spots

    def yes(condition):
        return jnp.where(condition, 1, 0)

    is_a = (gx == 9) | (gx == 11) | (gx == 13) | (gx == 14)
    is_b = (gx == 1) | (gx == 3) | (gx == 5) | (gx == 7)
    near_count = 3 - yes(at_step)
    expected = near_count - 1 + 4 * yes(is_source) + yes(is_a) + yes(is_b)
    expected += yes(has_right) * jnp.where(gx == 7, 3, near_count)
    expected += yes(has_left) * jnp.where(gx == 8, 3, near_count)
    expected += 15 * yes(at_step & (gx == speaker))
    expected += yes(is_a & (gx >= 11) & last_z) + yes(is_a & (gx <= 13) & first_z)
    expected += yes(is_b & (gx >= 3) & not_last) + yes(is_b & (gx <= 5) & not_first)
    pl.semaphore_wait(barrier, expected)
    for k in range(8):
        @pl.when(at_step & (gx == speaker) & (gx != half + k))
        def _(k=k):
            pl.semaphore_signal(go_sem, inc=1, device_id=(half + k, gy), device_id_type=MESH)

    at_ra, at_rb, at_rbl, at_rbr, at_p = 16, 16 + SUB, 16 + 2 * SUB, 16 + 3 * SUB, 16 + 4 * SUB
    at_strip = at_p + ROWS * SUB
    pieces = [pl.ds(PIECE * j, PIECE) for j in range(SUB)]
    inner = [pl.ds(8 + PIECE * j, PIECE) for j in range(SUB)]

    for j in range(SUB):
        for c in range(4):
            send(is_source, at_ra + j, s_ref.at[c, :, pieces[j]], ra.at[:, pieces[j]], (near_source[c] + zero, gy))

    @pl.when(is_a)
    def _():
        for j in range(SUB):
            arrived(at_ra + j, ra.at[:, pieces[j]])
    target = gx - 8 + yes(gx == 14)
    for j in range(SUB):
        piece = ra.at[:, pieces[j]]
        send(is_a, at_rb + j, piece, rb.at[:, pieces[j]], (target, gy))
        send(is_a & (gx >= 11) & last_z, at_rbl + j, piece, rbl.at[:, pieces[j]], (target, up))
        send(is_a & (gx <= 13) & first_z, at_rbr + j, piece, rbr.at[:, pieces[j]], (target, down))
    mid = pl.ds(8, CX)
    def edge(first, rows, low, cells):
        src = s_ref.at[pl.ds(first, rows), :, pl.ds(0, cells) if low else pl.ds(CX - cells, cells)]
        return src, pl.ds(EX - 8, cells) if low else pl.ds(8 - cells, cells)

    halo = [
        (always, s_ref.at[pl.ds(1, 3)], u0.at[pl.ds(0, 3), :, mid], (gx, up), always, (0, 1)),
        (always, s_ref.at[pl.ds(0, 3)], u0.at[pl.ds(7, 3), :, mid], (gx, down), always, (2, 1)),
    ]
    for low in (False, True):
        condition, arrives, other, nx = (has_left, from_right, gx - 1, 2) if low else (has_right, from_left, gx + 1, 0)
        src, cells = edge(0, CY, low, HX)
        halo.append((condition, src, u0.at[pl.ds(HY, CY), :, cells], (other, gy), arrives, (1, nx)))
        src, cells = edge(2, 2, low, HX)
        halo.append((condition, src, u0.at[pl.ds(1, 2), :, cells], (other, up), arrives, (0, nx)))
        src, cells = edge(0, 2, low, HX)
        halo.append((condition, src, u0.at[pl.ds(7, 2), :, cells], (other, down), arrives, (2, nx)))
    receipts = []

    def send_halo(i, condition):
        wanted, src, dst, target, arrives, place = halo[i]
        copy = send(wanted & condition, i, src, dst, target)
        small = send(wanted & condition, 8 + i, dd, dn.at[place[0], place[1]], target)
        return [(arrives, copy), (arrives, small)]

    for i in range(len(halo)):
        far = last_z if i in (0, 3, 6) else first_z
        receipts += send_halo(i, always) if i in (2, 5) else send_halo(i, jnp.logical_not(far))
    def send_far(who):
        @pl.when(at_step & (gx != speaker) & who)
        def _():
            pl.semaphore_wait(go_sem, 1)

        for i in (0, 1, 3, 4, 6, 7):
            send_halo(i, (last_z if i in (0, 3, 6) else first_z) & who)

    send_far(always)

    for j in range(SUB):
        @pl.when(is_b)
        def _(j=j):
            arrived(at_rb + j, rb.at[:, pieces[j]])

        for c in range(4):
            row = HY + c
            here, piece = gx == near_fringe[c], rb.at[:, pieces[j]]
            send(here, at_p + row * SUB + j, piece, p0.at[row, :, inner[j]], (zero, gy))
            if c >= 1:
                send(here & not_last, at_p + (c - 1) * SUB + j, piece, p0.at[c - 1, :, inner[j]], (zero, up))
            if c <= 2:
                send(here & not_first, at_p + (7 + c) * SUB + j, piece, p0.at[7 + c, :, inner[j]], (zero, down))
    for j in range(SUB):
        @pl.when(is_b & (gx >= 3) & first_z)
        def _(j=j):
            arrived(at_rbl + j, rbl.at[:, pieces[j]])

        @pl.when(is_b & (gx <= 5) & last_z)
        def _(j=j):
            arrived(at_rbr + j, rbr.at[:, pieces[j]])

        for c in range(4):
            if c >= 1:
                row = c - 1
                send((gx == near_fringe[c]) & first_z, at_p + row * SUB + j, rbl.at[:, pieces[j]], p0.at[row, :, inner[j]], (zero, gy))
            if c <= 2:
                row = 7 + c
                send((gx == near_fringe[c]) & last_z, at_p + row * SUB + j, rbr.at[:, pieces[j]], p0.at[row, :, inner[j]], (zero, gy))

    @pl.when(gx == 0)
    def _():
        for j in range(SUB):
            for row in range(ROWS):
                arrived(at_p + row * SUB + j, p0.at[row, :, inner[j]])

    strip = pl.ds(1, 8)
    for k, (a, b) in enumerate(((64, 0), (8, 8))):
        copy = send(gx == 0, at_strip + k, p0.at[strip, :, pl.ds(a, 8)], p0.at[strip, :, pl.ds(b, 8)], (1 + zero, gy))

        @pl.when(gx == 1)
        def _(copy=copy):
            copy.wait_recv()

    lane = lax.broadcasted_iota(jnp.int32, (8, NZ), 1)
    low_edge, high_edge = lane == 0, lane == NZ - 1

    def terms(which, slot, row, t):
        cells, shifted = pl.ds(8 * t, 8), pl.ds(8 * t + 8, 8)
        u = [held[which][slot, row, f, cells] for f in range(NF)]
        inverse = 1.0 / u[0]
        speed = [u[1] * inverse, u[2] * inverse, u[3] * inverse]
        pressure = 0.4 * (u[4] - 0.5 * (u[1] * speed[0] + u[2] * speed[1] + u[3] * speed[2]))
        total = u[4] + pressure
        flux = []
        for d in range(3):
            part = [u[1 + d], u[1] * speed[d], u[2] * speed[d], u[3] * speed[d], total * speed[d]]
            part[1 + d] = part[1 + d] + pressure
            flux.append(part)
        if which == 0:
            force = thrust[row, cells] * u[1] * jnp.abs(speed[0])
        for f in range(NF):
            ax[row, f, shifted] = u[f] + flux[0][f]
            bx[row, f, shifted] = u[f] - flux[0][f]
            ay[row, f, cells] = u[f] + flux[1][f]
            by[row, f, cells] = u[f] - flux[1][f]
            a, b = u[f] + flux[2][f], u[f] - flux[2][f]
            vertical = jnp.where(low_edge, a, pltpu.roll(a, 1, 1)) + jnp.where(high_edge, b, pltpu.roll(b, NZ - 1, 1))
            rest = 0.5 * vertical - 3.0 * u[f]
            if which == 0 and f == 1:
                rest = rest + force
            if which == 0 and f == 4:
                rest = rest + force * speed[0]
            rr[row, f, cells] = rest

    def edge_terms(which, slot, row, t, sign, ref):
        cells = pl.ds(8 * t, 8)
        u = [held[which][slot, row, f, cells] for f in range(NF)]
        inverse = 1.0 / u[0]
        speed = u[2] * inverse
        square = (u[1] * u[1] + u[2] * u[2] + u[3] * u[3]) * inverse
        pressure = 0.4 * (u[4] - 0.5 * square)
        flux = [u[2], u[1] * speed, u[2] * speed + pressure, u[3] * speed, (u[4] + pressure) * speed]
        for f in range(NF):
            ref[row, f, cells] = u[f] + sign * flux[f]

    def update(which, slot, out, row, tiles, keep, take):
        for f in range(NF):
            done = []
            for t in range(tiles):
                cells = pl.ds(8 * t, 8)
                near = ax[row, f, pl.ds(8 * t + 7, 8)] + bx[row, f, pl.ds(8 * t + 9, 8)]
                near = near + (ay[row - 1, f, cells] + by[row + 1, f, cells])
                slope = 0.5 * near + rr[row, f, cells]
                fresh = held[which][slot, row, f, cells] + TIME_STEP * slope
                done.append(keep * held[which][0, row, f, cells] + take * fresh)
            for t in range(tiles):
                held[which][out, row, f, pl.ds(8 * t, 8)] = done[t]

    def advance(s, which, slot, out, tiles):
        keep = jnp.where(s == 0, 0.0, jnp.where(s == 1, 0.75, 1.0 / 3.0))
        take = jnp.where(s == 0, 1.0, jnp.where(s == 1, 0.25, 2.0 / 3.0))

        for t in range(tiles):
            edge_terms(which, slot, s, t, 1.0, ay)
        for t in range(tiles):
            edge_terms(which, slot, ROWS - 1 - s, t, -1.0, by)

        @pl.loop(s + 1, ROWS - 1 - s)
        def _(row):
            for t in range(tiles):
                terms(which, slot, row, t)

        if which == 0:
            @pl.when(gx == LAST - 1)
            def _():
                @pl.loop(s + 1, ROWS - 1 - s)
                def _(row):
                    bx[row, :, 80:81] = bx[row, :, 79:80]

        @pl.loop(s + 1, ROWS - 1 - s)
        def _(row):
            update(which, slot, out, row, tiles, keep, take)

    def precursor(tiles):
        def one(s, carry):
            advance(s, 1, s, s + 1, tiles)
            return carry

        lax.fori_loop(0, 3, one, 0)

    @pl.when(gx == 0)
    def _():
        @pl.loop(0, ROWS)
        def _(r):
            p0[r, :, 0:8] = p0[r, :, 64:72]
            p0[r, :, 72:80] = p0[r, :, 8:16]

        precursor(XT)

    @pl.when(gx == 1)
    def _():
        precursor(2)

    own.wait()
    for condition, copy in receipts:
        @pl.when(condition)
        def _(copy=copy):
            copy.wait_recv()
    for condition, copy in sends:
        @pl.when(condition)
        def _(copy=copy):
            copy.wait_send()

    @pl.when(gx == 0)
    def _():
        @pl.loop(0, ROWS)
        def _(r):
            u0[r, :, 0:8] = p0[r, :, 64:72]

    @pl.when(gx == LAST)
    def _():
        @pl.loop(0, ROWS)
        def _(r):
            u0[r, :, 0:8] = u0[r, :, 64:72]
            u0[r, :, 72:80] = u0[r, :, 8:16]

    lane_f = lane.astype(jnp.float32)
    sublane = lax.broadcasted_iota(jnp.int32, (8, NZ), 0)

    def disks(place, tile):
        line = dd if place == (1, 1) else dn.at[place[0], place[1]]
        wide = jnp.broadcast_to(line[tile // 2:tile // 2 + 1], (8, NZ))
        value = wide
        for k in range(8):
            shift = 64 * (tile % 2) + 8 * k
            if shift:
                value = jnp.where(sublane == k, pltpu.roll(wide, NZ - shift, 1), value)
        return value

    for ny in range(3):
        rows = {0: (1, 2, 3), 1: (0, 1, 2, 3), 2: (0, 1, 2)}[ny]
        base = {0: -1, 1: 3, 2: 7}[ny]
        for t in range(XT):
            if t == 0:
                spots = jnp.where(from_left, disks((ny, 0), CX // 8 - 1), -1.0)
            elif t == XT - 1:
                spots = jnp.where(from_right, disks((ny, 2), 0), -1.0)
            else:
                spots = disks((ny, 1), t - 1)
            for y in rows:
                one, two = spots[:, 2 * y:2 * y + 1], spots[:, 2 * y + 1:2 * y + 2]
                hit = (lane_f == one) | (lane_f == two)
                thrust[base + y, 8 * t:8 * t + 8] = jnp.where(hit, -0.5 * THRUST_COEFF, 0.0)

    def weights(tile):
        value = jnp.zeros((8, NZ), jnp.float32)
        for k in range(8):
            level = level_ref[8 * tile + k].astype(jnp.float32) / 64.0
            value = jnp.where(sublane == k, level, value)
        return value

    @pl.when(gx == 0)
    def _():
        wt[0:8] = jnp.ones((8, NZ), jnp.float32)
        for t in range(CX // 8):
            wt[8 + 8 * t:16 + 8 * t] = weights(t)

    @pl.when(gx == 1)
    def _():
        wt[0:8] = weights(CX // 8 - 1)

    def stage(s, carry):
        advance(s, 0, jnp.minimum(s, 1), 1, XT)

        def blend(tiles):
            @pl.loop(s + 1, ROWS - 1 - s)
            def _(row):
                for t in range(tiles):
                    cells = pl.ds(8 * t, 8)
                    weight = wt[cells]
                    for f in range(NF):
                        value = st[1, row, f, cells]
                        st[1, row, f, cells] = value + weight * (pp[s + 1, row, f, cells] - value)

        @pl.when(gx == 0)
        def _():
            blend(XT - 1)

        @pl.when(gx == 1)
        def _():
            blend(1)

        return carry

    lax.fori_loop(0, 3, stage, 0)
    for y in range(CY):
        o_ref[y] = st[1, HY + y, :, 8:8 + CX]


def shards(density, velocity, pressure, disk_cells, disk_count, fringe_level):
    with jax.named_scope("state"):
        fields = conserved_from(density, velocity, pressure)
        fields = jnp.transpose(fields, (2, 0, 1, 3))
    cells = disk_cells.reshape(4, NZ)
    vmem = pl.BlockSpec(memory_space=pltpu.VMEM)
    smem = pl.BlockSpec(memory_space=pltpu.SMEM)
    f32 = jnp.float32
    out = pl.pallas_call(
        body,
        out_shape=jax.ShapeDtypeStruct((CY, NF, CX, NZ), f32),
        in_specs=[vmem, vmem, smem, smem],
        out_specs=vmem,
        scratch_shapes=[
            pltpu.VMEM((2, ROWS, NF, EX, NZ), f32),
            pltpu.VMEM((4, ROWS, NF, EX, NZ), f32),
            pltpu.VMEM((ROWS, NF, EX + 16, NZ), f32),
            pltpu.VMEM((ROWS, NF, EX + 16, NZ), f32),
            pltpu.VMEM((ROWS, NF, EX, NZ), f32),
            pltpu.VMEM((ROWS, NF, EX, NZ), f32),
            pltpu.VMEM((ROWS, NF, EX, NZ), f32),
            pltpu.VMEM((ROWS, EX, NZ), f32),
            pltpu.VMEM((EX, NZ), f32),
            pltpu.VMEM((8, NZ), f32),
            pltpu.VMEM((3, 3, 8, NZ), f32),
            pltpu.VMEM((NF, CX, NZ), f32),
            pltpu.VMEM((NF, CX, NZ), f32),
            pltpu.VMEM((NF, CX, NZ), f32),
            pltpu.VMEM((NF, CX, NZ), f32),
            pltpu.SemaphoreType.REGULAR,
            pltpu.SemaphoreType.DMA,
            pltpu.SemaphoreType.DMA((220,)),
            pltpu.SemaphoreType.DMA((16 + (4 + ROWS) * SUB + 2,)),
        ],
        compiler_params=pltpu.CompilerParams(collective_id=0, has_side_effects=True),
    )(fields, cells, disk_count, fringe_level)
    return jnp.transpose(out, (1, 2, 0, 3))


def solution(mesh):
    in_specs = (
        P("gx", "gy", None),
        P(None, "gx", "gy", None),
        P("gx", "gy", None),
        P("gx", "gy", None),
        P("gx", "gy"),
        P(),
    )
    out_specs = P(None, "gx", "gy", None)
    return jax.shard_map(shards, mesh=mesh, in_specs=in_specs, out_specs=out_specs, check_vma=False)
```
